32 devices in a mesh: pages: 2 (over y), rows: 4 (over x, core), cols: 4 (over z).
Axes of the slice: x: 2, y: 2, z: 4, core: 2. Of those that a mesh axis runs over, the one named last changes fastest.
Arguments:
- features: bfloat16 [128, 64, 768], P(('pages', 'rows'), 'cols'), parts along dimension 0, may hold values from -6 to 6
- dw_kernel: bfloat16 [31, 31, 768], P(None, None, ('rows', 'cols')), may hold values from -0.1875 to 0.1875
- w_up: bfloat16 [768, 1536], P(None, ('rows', 'cols')), may hold values from -0.21875 to 0.21875
- w_down: bfloat16 [768, 1536], P(None, ('rows', 'cols')), may hold values from -0.15625 to 0.15625
Outputs:
- block_out: bfloat16 [128, 64, 768], P(('pages', 'rows'), 'cols'), parts along dimension 0
The draws below stay inside these ranges and needn't reach their ends.
There are 2 independent parts, one for each index of `pages`. The reference program is written for one: setup_inputs(seed, part) draws one part's arguments, and reference() takes and returns one part's arrays. A program takes and returns all parts, laid end to end along the dimension named above; an argument that names none is the same for every part. Nothing has to cross between parts.
All inputs are finite; a program needn't handle non-finite values.
Results may differ from the reference program's by a relative error of at most 0.0053.
Values may be sent and summed in bfloat16 or wider, within the bound.
No kernel may reach another device: no remote copies, remote signals or barrier semaphores. Data moves between devices by JAX's collectives and lax.ppermute only.
A program may use at most 64 MiB of HBM per device.

```python
import jax
import jax.numpy as jnp
from jax import lax

C = 768
FF = 1536
KS = 31
H = 64
W = 64


def steps_of(stream_key, dims, shards, smallest, high):
    def one(position, parts):
        steps = jax.random.uniform(jax.random.fold_in(jax.random.fold_in(stream_key, 6), position), (parts,), jnp.float32, smallest / len(shards), high / len(shards))
        return jnp.repeat(jnp.exp(steps), dims[position] // parts).reshape((-1,) + (1,) * (len(dims) - position - 1))

    loudness = one(*shards[0])
    for cut in shards[1:]:
        loudness = loudness * one(*cut)
    return loudness


def normal_values(stream_key, extent, width, limit, shards=(), kind=jnp.bfloat16):
    values = jax.random.normal(stream_key, extent, jnp.float32) * width
    if len(shards) > 0:
        values = steps_of(stream_key, extent, shards, -0.22, 0.18) * values
    return jnp.clip(values, min=-limit, max=limit).astype(kind)


def setup_inputs(seed: int = 0, part: int = 0) -> dict:
    seeds = jax.random.split(jax.random.key(seed), 5)
    part_splits = jax.random.split(jax.random.fold_in(seeds[4], part), 5)
    features = normal_values(part_splits[0], (H, W, C), 1.0, 6.0, ((0, 4), (1, 4)))
    dw_kernel = normal_values(seeds[1], (KS, KS, C), (KS * KS) ** -0.5, 0.1875, ((2, 16),))
    w_up = normal_values(seeds[2], (C, FF), C ** -0.5, 0.21875, ((1, 16),))
    w_down = normal_values(seeds[3], (C, FF), FF ** -0.5, 0.15625, ((1, 16),))
    return {"features": features, "dw_kernel": dw_kernel, "w_up": w_up, "w_down": w_down}


def reference(features, dw_kernel, w_up, w_down):
    half = (KS - 1) // 2
    padded = jnp.pad(features, ((half, half), (half, half), (0, 0)))
    kernel = dw_kernel.reshape(KS, KS, 1, C)
    mixed = lax.conv_general_dilated(padded[None], kernel, (1, 1), 'VALID', dimension_numbers=('NHWC', 'HWIO', 'NHWC'), feature_group_count=C, preferred_element_type=jnp.float32)[0]
    spread = (features.astype(jnp.float32) + mixed).astype(jnp.bfloat16)
    flat = spread.reshape(H * W, C)

    def one_block(rows_block):
        values = rows_block.astype(jnp.float32)
        center = lax.optimization_barrier(jnp.mean(values, axis=1, keepdims=True))
        spread_sq = lax.optimization_barrier(jnp.mean((values - center) ** 2, axis=1, keepdims=True))
        normed = ((values - center) * lax.rsqrt(spread_sq + 1e-06)).astype(jnp.bfloat16)
        hidden = jax.nn.gelu(jnp.dot(normed, w_up, preferred_element_type=jnp.float32), approximate=False).astype(jnp.bfloat16)
        ffn = lax.dot_general(hidden, w_down, (((1,), (1,)), ((), ())), preferred_element_type=jnp.float32)
        return (values + ffn).astype(jnp.bfloat16)
    blocks = flat.reshape(-1, 4096, C) if H * W % 4096 == 0 else flat.reshape(1, H * W, C)
    result = lax.map(one_block, blocks)
    return result.reshape(H, W, C)
```

```python
import jax
import jax.numpy as jnp
from jax import lax
from jax.experimental import pallas as pl
from jax.experimental.pallas import tpu as pltpu
from jax.sharding import PartitionSpec as P

LANES = 128
STEP = 8


def conv_kernel(v_ref, img_ref, out_ref, shifted, toeplitz, *, half, segs):
    _, height, width = img_ref.shape
    groups = v_ref.shape[2] * segs
    tiles = v_ref.shape[2]
    rows = height + STEP * (groups - 1)

    @pl.when(pl.program_id(0) == 0)
    def _():
        shifted[...] = jnp.zeros_like(shifted)

    cells_in = lax.broadcasted_iota(jnp.int32, (width, LANES), 0)
    cells_out = lax.broadcasted_iota(jnp.int32, (width, LANES), 1) % width
    band = jnp.abs(cells_in - cells_out) <= half

    x = img_ref[0].astype(jnp.float32)
    for seg in range(segs):
        shifted[half - seg : half - seg + height, seg * width : (seg + 1) * width] = x
    for shift in range(STEP):
        for tile in range(tiles):
            row = jnp.broadcast_to(
                v_ref[0, shift, tile : tile + 1, :].astype(jnp.float32), (width, LANES)
            )
            turned = pltpu.roll(row, LANES - half, axis=1, stride=1, stride_axis=0)
            toeplitz[
                shift * width : (shift + 1) * width, tile * LANES : (tile + 1) * LANES
            ] = jnp.where(band, turned, 0.0).astype(jnp.bfloat16)
    left = jnp.concatenate(
        [shifted[s : s + rows, :].astype(jnp.bfloat16) for s in range(0, STEP, segs)], axis=1
    )
    product = jnp.dot(left, toeplitz[...], preferred_element_type=jnp.float32)
    keep = height + STEP * (segs - 1)
    total = product[:keep, :LANES]
    for tile in range(1, tiles):
        start = tile * segs * STEP
        total = total + product[start : start + keep, tile * LANES : (tile + 1) * LANES]
    mixed = total[:height, :width]
    for seg in range(1, segs):
        part = total[seg * STEP : seg * STEP + height, :]
        mixed = mixed + pltpu.roll(part, LANES - seg * width, axis=1)[:, :width]
    out_ref[0] = (x + mixed).astype(out_ref.dtype)


def spread_of(taps, images):
    side, _, count = taps.shape
    half = (side - 1) // 2
    _, height, width = images.shape
    segs = LANES // width
    groups = -(-side // (STEP * segs)) * segs
    v = jnp.transpose(taps[:, ::-1, :], (2, 0, 1))
    v = jnp.pad(v, ((0, 0), (0, STEP * groups - side), (0, width - side)))
    v = v.reshape(count, groups, STEP, width).transpose(0, 2, 1, 3)
    v = v.reshape(count, STEP, groups // segs, LANES)
    return pl.pallas_call(
        lambda *refs: conv_kernel(*refs, half=half, segs=segs),
        grid=(count,),
        in_specs=[
            pl.BlockSpec((1,) + v.shape[1:], lambda i: (i, 0, 0, 0)),
            pl.BlockSpec((1, height, width), lambda i: (i, 0, 0)),
        ],
        out_specs=pl.BlockSpec((1, height, width), lambda i: (i, 0, 0)),
        out_shape=jax.ShapeDtypeStruct(images.shape, images.dtype),
        scratch_shapes=[
            pltpu.VMEM((height + STEP * groups, LANES), jnp.float32),
            pltpu.VMEM((STEP * width, groups * width), jnp.bfloat16),
        ],
        name="depthwise",
    )(v, images)


def on_device(features, dw_kernel, w_up, w_down):
    axes = ("rows", "cols")
    down = lax.axis_size("rows")
    across = lax.axis_size("cols")
    devices = down * across
    tile_rows, tile_cols, channels = features.shape
    cells = tile_rows * tile_cols
    own = channels // devices
    weights = jnp.concatenate([w_up.T, w_down.T], axis=0)
    weights = lax.all_gather(weights, axes, axis=0)
    piece = w_up.shape[1]
    turned = features.reshape(cells, channels).T.reshape(devices, own, cells)
    images = lax.all_to_all(turned, axes, 0, 0, tiled=True)
    images = images.reshape(down, across, own, tile_rows, tile_cols)
    images = images.transpose(2, 0, 3, 1, 4).reshape(own, down * tile_rows, across * tile_cols)
    spread = spread_of(dw_kernel, images)
    spread = spread.reshape(own, down, tile_rows, across, tile_cols)
    spread = spread.transpose(1, 3, 0, 2, 4).reshape(devices, own, cells)
    spread = lax.all_to_all(spread, axes, 0, 0, tiled=True)
    values = spread.reshape(channels, cells).T.astype(jnp.float32)
    center = jnp.mean(values, axis=1, keepdims=True)
    spread_sq = jnp.mean((values - center) ** 2, axis=1, keepdims=True)
    normed = ((values - center) * lax.rsqrt(spread_sq + 1e-06)).astype(jnp.bfloat16)
    up = weights[:, :piece].reshape(devices * piece, channels)
    back = weights[:, piece:].reshape(devices * piece, channels)
    hidden = jax.nn.gelu(
        lax.dot_general(
            normed, up, (((1,), (1,)), ((), ())), preferred_element_type=jnp.float32
        ),
        approximate=False,
    ).astype(jnp.bfloat16)
    ffn = jnp.dot(hidden, back, preferred_element_type=jnp.float32)
    result = (values + ffn).astype(jnp.bfloat16)
    return result.reshape(tile_rows, tile_cols, channels)


def solution(mesh):
    return jax.shard_map(
        on_device,
        mesh=mesh,
        in_specs=(
            P(("pages", "rows"), "cols", None),
            P(None, None, ("rows", "cols")),
            P(None, ("rows", "cols")),
            P(None, ("rows", "cols")),
        ),
        out_specs=P(("pages", "rows"), "cols", None),
        check_vma=False,
    )
```

```python
import jax
import jax.numpy as jnp
from jax import lax
from jax.experimental import pallas as pl
from jax.experimental.pallas import tpu as pltpu
from jax.sharding import PartitionSpec as P

LANES = 128
STEP = 8
BUILD = 8
CONV = 16


def per_step(count, most):
    return max(n for n in range(1, most + 1) if count % n == 0)


def toeplitz_kernel(v_ref, out_ref, *, half, width):
    count, steps, tiles, _ = v_ref.shape
    block = 16
    lane = lax.broadcasted_iota(jnp.int32, (block, LANES), 1) % width
    row = lax.broadcasted_iota(jnp.int32, (block, LANES), 0)
    bands = [jnp.abs(row + start - lane) <= half for start in range(0, width, block)]
    def build(channel, carry):
        for shift in range(steps):
            for tile in range(tiles):
                taps = v_ref[channel, shift, tile : tile + 1, :]
                taps = jnp.broadcast_to(taps.astype(jnp.float32), (block, LANES))
                turned = pltpu.roll(taps, LANES - half, axis=1, stride=1, stride_axis=0)
                for index, band in enumerate(bands):
                    start = index * block
                    piece = turned if start == 0 else pltpu.roll(turned, start, axis=1)
                    out_ref[
                        channel,
                        shift * width + start : shift * width + start + block,
                        tile * LANES : (tile + 1) * LANES,
                    ] = jnp.where(band, piece, 0.0).astype(jnp.bfloat16)
        return carry

    lax.fori_loop(0, count, build, 0)


def conv_kernel(matrix_ref, img_ref, out_ref, shifted, *, half, segs):
    count, height, width = img_ref.shape
    tiles = matrix_ref.shape[2] // LANES
    rows = height + STEP * (tiles * segs - 1)

    @pl.when(pl.program_id(0) == 0)
    def _():
        shifted[...] = jnp.zeros_like(shifted)

    for channel in range(count):
        x = img_ref[channel].astype(jnp.float32)
        for seg in range(segs):
            shifted[
                channel, half - seg : half - seg + height, seg * width : (seg + 1) * width
            ] = x
        left = jnp.concatenate(
            [
                shifted[channel, s : s + rows, :].astype(jnp.bfloat16)
                for s in range(0, STEP, segs)
            ],
            axis=1,
        )
        product = jnp.dot(left, matrix_ref[channel], preferred_element_type=jnp.float32)
        keep = height + STEP * (segs - 1)
        total = product[:keep, :LANES]
        for tile in range(1, tiles):
            start = tile * segs * STEP
            total = total + product[start : start + keep, tile * LANES : (tile + 1) * LANES]
        mixed = total[:height, :width]
        for seg in range(1, segs):
            part = total[seg * STEP : seg * STEP + height, :]
            mixed = mixed + pltpu.roll(part, LANES - seg * width, axis=1)[:, :width]
        out_ref[channel] = (x + mixed).astype(out_ref.dtype)


def matrices_of(taps, width):
    side, _, count = taps.shape
    half = (side - 1) // 2
    segs = LANES // width
    groups = -(-side // (STEP * segs)) * segs
    v = jnp.transpose(taps[:, ::-1, :], (2, 0, 1))
    v = jnp.pad(v, ((0, 0), (0, STEP * groups - side), (0, width - side)))
    v = v.reshape(count, groups, STEP, width).transpose(0, 2, 1, 3)
    v = v.reshape(count, STEP, groups // segs, LANES)
    several = per_step(count, BUILD)
    shape = (STEP * width, groups * width)
    return pl.pallas_call(
        lambda *refs: toeplitz_kernel(*refs, half=half, width=width),
        grid=(count // several,),
        in_specs=[pl.BlockSpec((several,) + v.shape[1:], lambda i: (i, 0, 0, 0))],
        out_specs=pl.BlockSpec((several,) + shape, lambda i: (i, 0, 0)),
        out_shape=jax.ShapeDtypeStruct((count,) + shape, taps.dtype),
        cost_estimate=pl.CostEstimate(
            flops=count * shape[0] * shape[1] * 4,
            transcendentals=0,
            bytes_accessed=count * shape[0] * shape[1] * 2,
        ),
        name="toeplitz",
    )(v)


def spread_of(matrices, images, half):
    count, height, width = images.shape
    segs = LANES // width
    groups = matrices.shape[2] // width
    several = per_step(count, CONV)
    return pl.pallas_call(
        lambda *refs: conv_kernel(*refs, half=half, segs=segs),
        grid=(count // several,),
        in_specs=[
            pl.BlockSpec((several,) + matrices.shape[1:], lambda i: (i, 0, 0)),
            pl.BlockSpec((several, height, width), lambda i: (i, 0, 0)),
        ],
        out_specs=pl.BlockSpec((several, height, width), lambda i: (i, 0, 0)),
        out_shape=jax.ShapeDtypeStruct(images.shape, images.dtype),
        scratch_shapes=[pltpu.VMEM((several, height + STEP * groups, LANES), jnp.float32)],
        name="depthwise",
    )(matrices, images)


def on_device(features, dw_kernel, w_up, w_down):
    axes = ("rows", "cols")
    down = lax.axis_size("rows")
    across = lax.axis_size("cols")
    devices = down * across
    tile_rows, tile_cols, channels = features.shape
    cells = tile_rows * tile_cols
    own = channels // devices
    weights = jnp.concatenate([w_up.T, w_down.T], axis=0)
    weights = lax.all_gather(weights, axes, axis=0)
    piece = w_up.shape[1]
    turned = features.reshape(cells, channels).T.reshape(devices, own, cells)
    matrices = matrices_of(dw_kernel, across * tile_cols)
    images = lax.all_to_all(turned, axes, 0, 0, tiled=True)
    images = images.reshape(down, across, own, tile_rows, tile_cols)
    images = images.transpose(2, 0, 3, 1, 4).reshape(own, down * tile_rows, across * tile_cols)
    spread = spread_of(matrices, images, (dw_kernel.shape[0] - 1) // 2)
    spread = spread.reshape(own, down, tile_rows, across, tile_cols)
    spread = spread.transpose(1, 3, 0, 2, 4).reshape(devices, own, cells)
    spread = lax.all_to_all(spread, axes, 0, 0, tiled=True)
    values = spread.reshape(channels, cells).T.astype(jnp.float32)
    center = jnp.mean(values, axis=1, keepdims=True)
    spread_sq = jnp.mean((values - center) ** 2, axis=1, keepdims=True)
    normed = ((values - center) * lax.rsqrt(spread_sq + 1e-06)).astype(jnp.bfloat16)
    up = weights[:, :piece].reshape(devices * piece, channels)
    back = weights[:, piece:].reshape(devices * piece, channels)
    hidden = jax.nn.gelu(
        lax.dot_general(
            normed, up, (((1,), (1,)), ((), ())), preferred_element_type=jnp.float32
        ),
        approximate=False,
    ).astype(jnp.bfloat16)
    ffn = jnp.dot(hidden, back, preferred_element_type=jnp.float32)
    result = (values + ffn).astype(jnp.bfloat16)
    return result.reshape(tile_rows, tile_cols, channels)


def solution(mesh):
    return jax.shard_map(
        on_device,
        mesh=mesh,
        in_specs=(
            P(("pages", "rows"), "cols", None),
            P(None, None, ("rows", "cols")),
            P(None, ("rows", "cols")),
            P(None, ("rows", "cols")),
        ),
        out_specs=P(("pages", "rows"), "cols", None),
        check_vma=False,
    )
```

```python
import jax
import jax.numpy as jnp
from jax import lax
from jax.experimental import pallas as pl
from jax.experimental.pallas import tpu as pltpu
from jax.sharding import PartitionSpec as P

LANES = 128
STEP = 8
BUILD = 8
CONV = 16


def per_step(count, most):
    return max(n for n in range(1, most + 1) if count % n == 0)


def toeplitz_kernel(v_ref, out_ref, *, half, width):
    count, steps, tiles, _ = v_ref.shape
    block = 16
    lane = lax.broadcasted_iota(jnp.int32, (block, LANES), 1) % width
    row = lax.broadcasted_iota(jnp.int32, (block, LANES), 0)
    bands = [jnp.abs(row + start - lane) <= half for start in range(0, width, block)]

    def build(channel, carry):
        for shift in range(steps):
            for tile in range(tiles):
                taps = v_ref[channel, shift, tile : tile + 1, :]
                taps = jnp.broadcast_to(taps.astype(jnp.float32), (block, LANES))
                turned = pltpu.roll(taps, LANES - half, axis=1, stride=1, stride_axis=0)
                for index, band in enumerate(bands):
                    start = index * block
                    piece = turned if start == 0 else pltpu.roll(turned, start, axis=1)
                    out_ref[
                        channel,
                        shift * width + start : shift * width + start + block,
                        tile * LANES : (tile + 1) * LANES,
                    ] = jnp.where(band, piece, 0.0).astype(jnp.bfloat16)
        return carry

    lax.fori_loop(0, count, build, 0)


def conv_kernel(matrix_ref, img_ref, out_ref, shifted, *, half, segs):
    count, height, width = img_ref.shape
    tiles = matrix_ref.shape[2] // LANES
    rows = height + STEP * (tiles * segs - 1)

    @pl.when(pl.program_id(0) == 0)
    def _():
        shifted[...] = jnp.zeros_like(shifted)

    for channel in range(count):
        x = img_ref[channel].astype(jnp.float32)
        for seg in range(segs):
            shifted[
                channel, half - seg : half - seg + height, seg * width : (seg + 1) * width
            ] = x
        left = jnp.concatenate(
            [
                shifted[channel, s : s + rows, :].astype(jnp.bfloat16)
                for s in range(0, STEP, segs)
            ],
            axis=1,
        )
        product = jnp.dot(left, matrix_ref[channel], preferred_element_type=jnp.float32)
        keep = height + STEP * (segs - 1)
        total = product[:keep, :LANES]
        for tile in range(1, tiles):
            start = tile * segs * STEP
            total = total + product[start : start + keep, tile * LANES : (tile + 1) * LANES]
        mixed = total[:height, :width]
        for seg in range(1, segs):
            part = total[seg * STEP : seg * STEP + height, :]
            mixed = mixed + pltpu.roll(part, LANES - seg * width, axis=1)[:, :width]
        out_ref[channel] = (x + mixed).astype(out_ref.dtype)


def matrices_of(taps, width):
    side, _, count = taps.shape
    half = (side - 1) // 2
    segs = LANES // width
    groups = -(-side // (STEP * segs)) * segs
    v = jnp.transpose(taps[:, ::-1, :], (2, 0, 1))
    v = jnp.pad(v, ((0, 0), (0, STEP * groups - side), (0, width - side)))
    v = v.reshape(count, groups, STEP, width).transpose(0, 2, 1, 3)
    v = v.reshape(count, STEP, groups // segs, LANES)
    several = per_step(count, BUILD)
    shape = (STEP * width, groups * width)
    return pl.pallas_call(
        lambda *refs: toeplitz_kernel(*refs, half=half, width=width),
        grid=(count // several,),
        in_specs=[pl.BlockSpec((several,) + v.shape[1:], lambda i: (i, 0, 0, 0))],
        out_specs=pl.BlockSpec((several,) + shape, lambda i: (i, 0, 0)),
        out_shape=jax.ShapeDtypeStruct((count,) + shape, taps.dtype),
        cost_estimate=pl.CostEstimate(
            flops=count * shape[0] * shape[1] * 4,
            transcendentals=0,
            bytes_accessed=count * shape[0] * shape[1] * 2,
        ),
        name="toeplitz",
    )(v)


def spread_of(matrices, images, half):
    count, height, width = images.shape
    segs = LANES // width
    groups = matrices.shape[2] // width
    several = per_step(count, CONV)
    return pl.pallas_call(
        lambda *refs: conv_kernel(*refs, half=half, segs=segs),
        grid=(count // several,),
        in_specs=[
            pl.BlockSpec((several,) + matrices.shape[1:], lambda i: (i, 0, 0)),
            pl.BlockSpec((several, height, width), lambda i: (i, 0, 0)),
        ],
        out_specs=pl.BlockSpec((several, height, width), lambda i: (i, 0, 0)),
        out_shape=jax.ShapeDtypeStruct(images.shape, images.dtype),
        scratch_shapes=[pltpu.VMEM((several, height + STEP * groups, LANES), jnp.float32)],
        name="depthwise",
    )(matrices, images)


def add_hidden(total, normed, piece_refs):
    for ref in piece_refs:
        count, _, units, channels = ref.shape
        up = ref[:, 0].reshape(count * units, channels)
        down = ref[:, 1].reshape(count * units, channels)
        hidden = lax.dot_general(
            normed, up, (((1,), (1,)), ((), ())), preferred_element_type=jnp.float32
        )
        hidden = (0.5 * hidden * (1.0 + lax.erf(hidden * 0.5**0.5))).astype(jnp.bfloat16)
        total = total + jnp.dot(hidden, down, preferred_element_type=jnp.float32)
    return total


def first_kernel(*refs):
    spread_ref, *piece_refs, normed_ref, total_ref = refs
    values = spread_ref[...].astype(jnp.float32).T
    center = jnp.mean(values, axis=1, keepdims=True)
    spread_sq = jnp.mean((values - center) ** 2, axis=1, keepdims=True)
    normed = ((values - center) * lax.rsqrt(spread_sq + 1e-06)).astype(jnp.bfloat16)
    normed_ref[...] = normed
    total_ref[...] = add_hidden(values, normed, piece_refs)


def second_kernel(*refs):
    normed_ref, total_ref, *piece_refs, out_ref = refs
    total = add_hidden(total_ref[...], normed_ref[...], piece_refs)
    out_ref[...] = total.astype(out_ref.dtype)


def aligned(pieces):
    channels = pieces[0].shape[3]
    if pieces[0].shape[2] % 16 != 0:
        joined = jnp.concatenate(pieces, axis=0)
        pieces = [joined.transpose(1, 0, 2, 3).reshape(1, 2, -1, channels)]
    return pieces


def block_of(spread, near, far):
    channels, cells = spread.shape
    near, far = aligned(near), aligned(far)
    whole = pl.BlockSpec(memory_space=pltpu.VMEM)
    normed, total = pl.pallas_call(
        first_kernel,
        in_specs=[whole] * (1 + len(near)),
        out_specs=[whole] * 2,
        out_shape=[
            jax.ShapeDtypeStruct((cells, channels), spread.dtype),
            jax.ShapeDtypeStruct((cells, channels), jnp.float32),
        ],
        name="feed_forward_near",
    )(spread, *near)
    return pl.pallas_call(
        second_kernel,
        in_specs=[whole] * (2 + len(far)),
        out_specs=whole,
        out_shape=jax.ShapeDtypeStruct((cells, channels), spread.dtype),
        name="feed_forward_far",
    )(normed, total, *far)


def turn(array, axis, shift, within=1):
    size = lax.axis_size(axis)
    return lax.ppermute(
        array, axis, [(i, (i + shift * within) % size) for i in range(size)]
    )


def partner(array, axis):
    size = lax.axis_size(axis)
    return lax.ppermute(array, axis, [(i, i ^ 1) for i in range(size)])


def on_device(features, dw_kernel, w_up, w_down):
    axes = ("rows", "cols")
    down = lax.axis_size("rows")
    across = lax.axis_size("cols")
    devices = down * across
    tile_rows, tile_cols, channels = features.shape
    cells = tile_rows * tile_cols
    own = channels // devices
    pages = lax.axis_size("pages")
    units = w_up.shape[1] // pages
    piece = jnp.stack([w_up.T, w_down.T])[None]
    piece = lax.dynamic_slice_in_dim(piece, lax.axis_index("pages") * units, units, axis=2)
    line = [piece] + [turn(piece, "cols", shift) for shift in range(1, across)]
    turned = features.reshape(cells, channels).T.reshape(devices, own, cells)
    images = lax.all_to_all(turned, axes, 0, 0, tiled=True)
    matrices = matrices_of(dw_kernel, across * tile_cols)
    images, matrices, line = lax.optimization_barrier((images, matrices, line))
    line = jnp.concatenate(line, axis=0)
    others = [turn(line, "rows", shift, 2) for shift in range(1, down // 2)]
    near = [line] + [turn(line, "pages", shift) for shift in range(1, pages)]
    images = images.reshape(down, across, own, tile_rows, tile_cols)
    images = images.transpose(2, 0, 3, 1, 4).reshape(own, down * tile_rows, across * tile_cols)
    spread = spread_of(matrices, images, (dw_kernel.shape[0] - 1) // 2)
    spread = spread.reshape(own, down, tile_rows, across, tile_cols)
    spread = spread.transpose(1, 3, 0, 2, 4).reshape(devices, own, cells)
    spread, others, near = lax.optimization_barrier((spread, others, near))
    near = near + others
    far = [partner(each, "rows") for each in near]
    last = [turn(other, "pages", shift) for other in others for shift in range(1, pages)]
    spread = lax.all_to_all(spread, axes, 0, 0, tiled=True)
    spread, last = lax.optimization_barrier((spread, last))
    far += [partner(each, "rows") for each in last]
    result = block_of(spread.reshape(channels, cells), near + last, far)
    return result.reshape(tile_rows, tile_cols, channels)


def solution(mesh):
    return jax.shard_map(
        on_device,
        mesh=mesh,
        in_specs=(
            P(("pages", "rows"), "cols", None),
            P(None, None, ("rows", "cols")),
            P(None, ("rows", "cols")),
            P(None, ("rows", "cols")),
        ),
        out_specs=P(("pages", "rows"), "cols", None),
        check_vma=False,
    )
```

```python
import jax
import jax.numpy as jnp
from jax import lax
from jax.experimental import pallas as pl
from jax.experimental.pallas import tpu as pltpu
from jax.sharding import PartitionSpec as P


LANES = 128
STEP = 8
BUILD = 8
CONV = 16
CHUNK = 8


def per_step(count, most):
    return max(n for n in range(1, most + 1) if count % n == 0)


def toeplitz_kernel(v_ref, out_ref, *, half, width):
    count, steps, tiles, _ = v_ref.shape
    block = 16
    lane = lax.broadcasted_iota(jnp.int32, (block, LANES), 1) % width
    row = lax.broadcasted_iota(jnp.int32, (block, LANES), 0)
    bands = [
        jnp.where(jnp.abs(row + start - lane) <= half, 1.0, 0.0).astype(jnp.bfloat16)
        for start in range(0, width, block)
    ]

    def build(channel, carry):
        for shift in range(steps):
            for tile in range(tiles):
                taps = v_ref[channel, shift, tile : tile + 1, :]
                taps = jnp.broadcast_to(taps.astype(jnp.float32), (block, LANES))
                turned = pltpu.roll(taps, LANES - half, axis=1, stride=1, stride_axis=0)
                turned = turned.astype(jnp.bfloat16)
                for index, band in enumerate(bands):
                    start = index * block
                    piece = turned if start == 0 else pltpu.roll(turned, start, axis=1)
                    low = shift * width + start
                    out_ref[channel, tile, low : low + block, :] = piece * band
        return carry

    lax.fori_loop(0, count, build, 0)


def conv_kernel(matrix_ref, img_ref, out_ref, shifted, *, half, segs):
    count, height, width = img_ref.shape
    tiles = matrix_ref.shape[1]
    rows = height + STEP * (tiles * segs - 1)

    @pl.when(pl.program_id(0) == 0)
    def _():
        shifted[...] = jnp.zeros_like(shifted)

    for channel in range(count):
        x = img_ref[channel].astype(jnp.float32)
        for seg in range(segs):
            shifted[
                channel, half - seg : half - seg + height, seg * width : (seg + 1) * width
            ] = x
        left = jnp.concatenate(
            [
                shifted[channel, s : s + rows, :].astype(jnp.bfloat16)
                for s in range(0, STEP, segs)
            ],
            axis=1,
        )
        matrix = jnp.concatenate([matrix_ref[channel, t] for t in range(tiles)], axis=1)
        product = jnp.dot(left, matrix, preferred_element_type=jnp.float32)
        keep = height + STEP * (segs - 1)
        total = product[:keep, :LANES]
        for tile in range(1, tiles):
            start = tile * segs * STEP
            total = total + product[start : start + keep, tile * LANES : (tile + 1) * LANES]
        mixed = total[:height, :width]
        for seg in range(1, segs):
            part = total[seg * STEP : seg * STEP + height, :]
            mixed = mixed + pltpu.roll(part, LANES - seg * width, axis=1)[:, :width]
        out_ref[channel] = (x + mixed).astype(out_ref.dtype)


def moved_kernel(
    recv_ref, into_ref, back_ref, matrix_hbm, out_ref, shifted, result, matrices, sems, *, half, segs
):
    count = recv_ref.shape[1]
    across = into_ref.shape[0] // LANES
    parts = recv_ref.shape[2] // LANES
    down = recv_ref.shape[0] // across
    chunks, chunk, tiles = matrices.shape[:3]
    width = LANES // segs
    taken = into_ref.shape[1] // LANES
    height = down * parts * taken
    pitch = shifted.shape[0] // count
    rows = height + STEP * (tiles * segs - 1)
    copies = [
        pltpu.make_async_copy(
            matrix_hbm.at[pl.ds(index * chunk, chunk)], matrices.at[index], sems.at[index]
        )
        for index in range(chunks)
    ]
    for copy in copies:
        copy.start()
    shifted[...] = jnp.zeros_like(shifted)
    left = jnp.concatenate(
        [
            jnp.concatenate(
                [
                    recv_ref[r * across + c, :, part * LANES : (part + 1) * LANES]
                    for c in range(across)
                ],
                axis=1,
            )
            for r in range(down)
            for part in range(parts)
        ],
        axis=0,
    )
    images = jnp.dot(left, into_ref[...], preferred_element_type=jnp.float32)
    for group in range(down * parts):
        for step in range(taken):
            row = half + group * taken + step
            shifted[pl.ds(row, count, stride=pitch), :] = images[
                group * count : (group + 1) * count, step * LANES : (step + 1) * LANES
            ]
    first = lax.broadcasted_iota(jnp.int32, (rows, LANES), 1) // width
    for channel in range(count):
        if channel % chunk == 0:
            copies[channel // chunk].wait()
        base = channel * pitch
        pieces = []
        for shift in range(0, STEP, segs):
            piece = shifted[base + shift : base + shift + rows, :]
            for seg in range(1, segs):
                low = base + shift + seg
                piece = jnp.where(first == seg, shifted[low : low + rows, :], piece)
            pieces.append(piece.astype(jnp.bfloat16))
        matrix = [matrices[channel // chunk, channel % chunk, tile] for tile in range(tiles)]
        product = jnp.dot(
            jnp.concatenate(pieces, axis=1),
            jnp.concatenate(matrix, axis=1),
            preferred_element_type=jnp.float32,
        )
        keep = height + STEP * (segs - 1)
        total = product[:keep, :LANES]
        for tile in range(1, tiles):
            start = tile * segs * STEP
            total = total + product[start : start + keep, tile * LANES : (tile + 1) * LANES]
        mixed = total[:height, :]
        for seg in range(1, segs):
            part = total[seg * STEP : seg * STEP + height, :]
            mixed = mixed + pltpu.roll(part, LANES - seg * width, axis=1)
        x = shifted[base + half : base + half + height, :]
        result[channel * height : (channel + 1) * height, :] = x + mixed
    left = jnp.concatenate(
        [
            jnp.concatenate(
                [
                    result[pl.ds(group * taken + step, count, stride=height), :].astype(
                        jnp.bfloat16
                    )
                    for step in range(taken)
                ],
                axis=1,
            )
            for group in range(down * parts)
        ],
        axis=0,
    )
    moved = jnp.dot(left, back_ref[...], preferred_element_type=jnp.float32)
    for r in range(down):
        for part in range(parts):
            group = r * parts + part
            for c in range(across):
                out_ref[r * across + c, :, part * LANES : (part + 1) * LANES] = moved[
                    group * count : (group + 1) * count, c * LANES : (c + 1) * LANES
                ].astype(out_ref.dtype)


def moves_of(across, tile_cols):
    taken = LANES // tile_cols
    width = across * tile_cols
    lane = jnp.arange(across * LANES)
    step, col = lane % LANES // tile_cols, lane // LANES * tile_cols + lane % tile_cols
    cell = jnp.arange(taken * LANES)
    same = step[:, None] == (cell // LANES)[None, :]
    into = same & (col[:, None] == (cell % LANES % width)[None, :])
    back = same & (col[:, None] == (cell % LANES)[None, :])
    return into.astype(jnp.bfloat16), back.T.astype(jnp.bfloat16)


def spread_moved(matrices, moves, received, half, across, tile_cols):
    devices, count, cells = received.shape
    segs = LANES // (across * tile_cols)
    height = devices // across * cells // tile_cols
    tiles = matrices.shape[1]
    pitch = height + STEP * tiles * segs
    chunk = per_step(count, CHUNK)
    whole = pl.BlockSpec(memory_space=pltpu.VMEM)
    return pl.pallas_call(
        lambda *refs: moved_kernel(*refs, half=half, segs=segs),
        in_specs=[whole] * 3 + [pl.BlockSpec(memory_space=pl.ANY)],
        out_specs=whole,
        out_shape=jax.ShapeDtypeStruct(received.shape, received.dtype),
        scratch_shapes=[
            pltpu.VMEM((count * pitch, LANES), jnp.float32),
            pltpu.VMEM((count * height, LANES), jnp.float32),
            pltpu.VMEM((count // chunk, chunk) + matrices.shape[1:], matrices.dtype),
            pltpu.SemaphoreType.DMA((count // chunk,)),
        ],
        name="depthwise_moved",
    )(received, *moves, matrices)


def matrices_of(taps, width):
    side, _, count = taps.shape
    half = (side - 1) // 2
    segs = LANES // width
    groups = -(-side // (STEP * segs)) * segs
    v = jnp.transpose(taps[:, ::-1, :], (2, 0, 1))
    v = jnp.pad(v, ((0, 0), (0, STEP * groups - side), (0, width - side)))
    v = v.reshape(count, groups, STEP, width).transpose(0, 2, 1, 3)
    v = v.reshape(count, STEP, groups // segs, LANES)
    several = per_step(count, BUILD)
    shape = (groups // segs, STEP * width, LANES)
    return pl.pallas_call(
        lambda *refs: toeplitz_kernel(*refs, half=half, width=width),
        grid=(count // several,),
        in_specs=[pl.BlockSpec((several,) + v.shape[1:], lambda i: (i, 0, 0, 0))],
        out_specs=pl.BlockSpec((several,) + shape, lambda i: (i, 0, 0, 0)),
        out_shape=jax.ShapeDtypeStruct((count,) + shape, taps.dtype),
        cost_estimate=pl.CostEstimate(
            flops=count * groups * STEP * width * width * 4,
            transcendentals=0,
            bytes_accessed=count * groups * STEP * width * width * 2,
        ),
        name="toeplitz",
    )(v)


def spread_of(matrices, images, half):
    count, height, width = images.shape
    segs = LANES // width
    groups = matrices.shape[1] * segs
    several = per_step(count, CONV)
    return pl.pallas_call(
        lambda *refs: conv_kernel(*refs, half=half, segs=segs),
        grid=(count // several,),
        in_specs=[
            pl.BlockSpec((several,) + matrices.shape[1:], lambda i: (i, 0, 0, 0)),
            pl.BlockSpec((several, height, width), lambda i: (i, 0, 0)),
        ],
        out_specs=pl.BlockSpec((several, height, width), lambda i: (i, 0, 0)),
        out_shape=jax.ShapeDtypeStruct(images.shape, images.dtype),
        scratch_shapes=[pltpu.VMEM((several, height + STEP * groups, LANES), jnp.float32)],
        name="depthwise",
    )(matrices, images)


def add_hidden(total, normed, piece_refs):
    for ref in piece_refs:
        count, _, units, channels = ref.shape
        up = ref[:, 0].reshape(count * units, channels)
        down = ref[:, 1].reshape(count * units, channels)
        hidden = lax.dot_general(
            normed, up, (((1,), (1,)), ((), ())), preferred_element_type=jnp.float32
        )
        hidden = (0.5 * hidden * (1.0 + lax.erf(hidden * 0.5**0.5))).astype(jnp.bfloat16)
        total = total + jnp.dot(hidden, down, preferred_element_type=jnp.float32)
    return total


def first_kernel(*refs):
    spread_ref, *piece_refs, normed_ref, total_ref = refs
    values = spread_ref[...].astype(jnp.float32).T
    center = jnp.mean(values, axis=1, keepdims=True)
    spread_sq = jnp.mean((values - center) ** 2, axis=1, keepdims=True)
    normed = ((values - center) * lax.rsqrt(spread_sq + 1e-06)).astype(jnp.bfloat16)
    normed_ref[...] = normed
    total_ref[...] = add_hidden(values, normed, piece_refs)


def second_kernel(*refs):
    normed_ref, total_ref, *piece_refs, out_ref = refs
    total = add_hidden(total_ref[...], normed_ref[...], piece_refs)
    out_ref[...] = total.astype(out_ref.dtype)


def aligned(pieces):
    channels = pieces[0].shape[3]
    if pieces[0].shape[2] % 16 != 0:
        joined = jnp.concatenate(pieces, axis=0)
        pieces = [joined.transpose(1, 0, 2, 3).reshape(1, 2, -1, channels)]
    return pieces


def block_of(spread, near, far):
    channels, cells = spread.shape
    near, far = aligned(near), aligned(far)
    whole = pl.BlockSpec(memory_space=pltpu.VMEM)
    normed, total = pl.pallas_call(
        first_kernel,
        in_specs=[whole] * (1 + len(near)),
        out_specs=[whole] * 2,
        out_shape=[
            jax.ShapeDtypeStruct((cells, channels), spread.dtype),
            jax.ShapeDtypeStruct((cells, channels), jnp.float32),
        ],
        name="feed_forward_near",
    )(spread, *near)
    return pl.pallas_call(
        second_kernel,
        in_specs=[whole] * (2 + len(far)),
        out_specs=whole,
        out_shape=jax.ShapeDtypeStruct((cells, channels), spread.dtype),
        name="feed_forward_far",
    )(normed, total, *far)


def turn(array, axis, shift, within=1):
    size = lax.axis_size(axis)
    return lax.ppermute(
        array, axis, [(i, (i + shift * within) % size) for i in range(size)]
    )


def partner(array, axis):
    size = lax.axis_size(axis)
    return lax.ppermute(array, axis, [(i, i ^ 1) for i in range(size)])


def on_tile(features, dw_kernel, w_up, w_down):
    axes = ("rows", "cols")
    down = lax.axis_size("rows")
    across = lax.axis_size("cols")
    pages = lax.axis_size("pages")
    devices = down * across
    tile_rows, tile_cols, channels = features.shape
    cells = tile_rows * tile_cols
    own = channels // devices
    half = (dw_kernel.shape[0] - 1) // 2
    units = w_up.shape[1] // pages
    piece = jnp.stack([w_up.T, w_down.T])[None]
    piece = lax.dynamic_slice_in_dim(piece, lax.axis_index("pages") * units, units, axis=2)
    line = [piece] + [turn(piece, "cols", shift) for shift in range(1, across)]
    turned = features.reshape(cells, channels).T.reshape(devices, own, cells)
    images = lax.all_to_all(turned, axes, 0, 0, tiled=True)
    matrices = matrices_of(dw_kernel, across * tile_cols)
    moves = moves_of(across, tile_cols)
    images, matrices, moves, line = lax.optimization_barrier((images, matrices, moves, line))
    line = jnp.concatenate(line, axis=0)
    others = [turn(line, "rows", shift, 2) for shift in range(1, down // 2)]
    near = [line] + [turn(line, "pages", shift) for shift in range(1, pages)]
    if own % 16 == 0:
        spread = spread_moved(matrices, moves, images, half, across, tile_cols)
    else:
        images = images.reshape(down, across, own, tile_rows, tile_cols)
        images = images.transpose(2, 0, 3, 1, 4)
        images = images.reshape(own, down * tile_rows, across * tile_cols)
        spread = spread_of(matrices, images, half)
        spread = spread.reshape(own, down, tile_rows, across, tile_cols)
        spread = spread.transpose(1, 3, 0, 2, 4).reshape(devices, own, cells)
    last = [turn(other, "pages", shift) for other in others for shift in range(1, pages)]
    near = near + others
    far = [partner(each, "rows") for each in near]
    spread = lax.all_to_all(spread, axes, 0, 0, tiled=True)
    spread, last = lax.optimization_barrier((spread, last))
    far += [partner(each, "rows") for each in last]
    result = block_of(spread.reshape(channels, cells), near + last, far)
    return result.reshape(tile_rows, tile_cols, channels)


def solution(mesh):
    return jax.shard_map(
        on_tile,
        mesh=mesh,
        in_specs=(
            P(("pages", "rows"), "cols", None),
            P(None, None, ("rows", "cols")),
            P(None, ("rows", "cols")),
            P(None, ("rows", "cols")),
        ),
        out_specs=P(("pages", "rows"), "cols", None),
        check_vma=False,
    )
```

```python
import jax
import jax.numpy as jnp
import numpy as np
from jax import lax
from jax.experimental import pallas as pl
from jax.experimental.pallas import tpu as pltpu
from jax.sharding import PartitionSpec as P


LANES = 128
STEP = 8
BUILD = 8
CONV = 16
CHUNK = 8


def per_step(count, most):
    return max(n for n in range(1, most + 1) if count % n == 0)


def toeplitz_kernel(v_ref, out_ref, *, half, width):
    count, steps, tiles, _ = v_ref.shape
    block = 16
    lane = lax.broadcasted_iota(jnp.int32, (block, LANES), 1) % width
    row = lax.broadcasted_iota(jnp.int32, (block, LANES), 0)
    bands = [
        jnp.where(jnp.abs(row + start - lane) <= half, 1.0, 0.0).astype(jnp.bfloat16)
        for start in range(0, width, block)
    ]

    def build(channel, carry):
        for shift in range(steps):
            for tile in range(tiles):
                taps = v_ref[channel, shift, tile : tile + 1, :]
                taps = jnp.broadcast_to(taps.astype(jnp.float32), (block, LANES))
                turned = pltpu.roll(taps, LANES - half, axis=1, stride=1, stride_axis=0)
                turned = turned.astype(jnp.bfloat16)
                for index, band in enumerate(bands):
                    start = index * block
                    piece = turned if start == 0 else pltpu.roll(turned, start, axis=1)
                    low = shift * width + start
                    out_ref[channel, tile, low : low + block, :] = piece * band
        return carry

    lax.fori_loop(0, count, build, 0, unroll=per_step(count, 2))


def conv_kernel(matrix_ref, img_ref, out_ref, shifted, *, half, segs):
    count, height, width = img_ref.shape
    tiles = matrix_ref.shape[1]
    rows = height + STEP * (tiles * segs - 1)

    @pl.when(pl.program_id(0) == 0)
    def _():
        shifted[...] = jnp.zeros_like(shifted)

    for channel in range(count):
        x = img_ref[channel].astype(jnp.float32)
        for seg in range(segs):
            shifted[
                channel, half - seg : half - seg + height, seg * width : (seg + 1) * width
            ] = x
        left = jnp.concatenate(
            [
                shifted[channel, s : s + rows, :].astype(jnp.bfloat16)
                for s in range(0, STEP, segs)
            ],
            axis=1,
        )
        matrix = jnp.concatenate([matrix_ref[channel, t] for t in range(tiles)], axis=1)
        product = jnp.dot(left, matrix, preferred_element_type=jnp.float32)
        keep = height + STEP * (segs - 1)
        total = product[:keep, :LANES]
        for tile in range(1, tiles):
            start = tile * segs * STEP
            total = total + product[start : start + keep, tile * LANES : (tile + 1) * LANES]
        mixed = total[:height, :width]
        for seg in range(1, segs):
            part = total[seg * STEP : seg * STEP + height, :]
            mixed = mixed + pltpu.roll(part, LANES - seg * width, axis=1)[:, :width]
        out_ref[channel] = (x + mixed).astype(out_ref.dtype)


def moved_kernel(*refs, half, segs):
    recv_ref, move_ref, *matrix_hbms = refs[:-5]
    out_ref, shifted, result, matrices, sems = refs[-5:]
    count = recv_ref.shape[1]
    across = move_ref.shape[0] // LANES
    parts = recv_ref.shape[2] // LANES
    down = recv_ref.shape[0] // across
    _, chunk, tiles = matrices.shape[:3]
    width = LANES // segs
    taken = move_ref.shape[1] // width
    height = down * parts * taken
    pitch = shifted.shape[0] // count
    rows = height + STEP * (tiles * segs - 1)
    sources = [
        matrix_hbm.at[pl.ds(start, chunk)]
        for matrix_hbm in matrix_hbms
        for start in range(0, matrix_hbm.shape[0], chunk)
    ]
    copies = [
        pltpu.make_async_copy(source, matrices.at[index], sems.at[index])
        for index, source in enumerate(sources)
    ]
    for copy in copies:
        copy.start()
    shifted[...] = jnp.zeros_like(shifted)
    left = jnp.concatenate(
        [
            jnp.concatenate(
                [
                    recv_ref[r * across + c, :, part * LANES : (part + 1) * LANES]
                    for c in range(across)
                ],
                axis=1,
            )
            for r in range(down)
            for part in range(parts)
        ],
        axis=0,
    )
    images = jnp.dot(left, move_ref[...], preferred_element_type=jnp.float32)
    place = lax.broadcasted_iota(jnp.int32, (count, LANES), 1) // width
    for group in range(down * parts):
        for block in range(taken // segs):
            value = images[
                group * count : (group + 1) * count, block * LANES : (block + 1) * LANES
            ]
            for seg in range(segs):
                spot = value
                for other in range(1, segs):
                    moved = pltpu.roll(value, other * width, axis=1)
                    spot = jnp.where(place == (seg + other) % segs, moved, spot)
                row = half + group * taken + block * segs + seg
                shifted[pl.ds(row, count, stride=pitch), :] = spot
    first = lax.broadcasted_iota(jnp.int32, (rows, LANES), 1) // width
    for channel in range(count):
        if channel % chunk == 0:
            copies[channel // chunk].wait()
        base = channel * pitch
        pieces = []
        for shift in range(0, STEP, segs):
            piece = shifted[base + shift : base + shift + rows, :]
            for seg in range(1, segs):
                low = base + shift + seg
                piece = jnp.where(first == seg, shifted[low : low + rows, :], piece)
            pieces.append(piece.astype(jnp.bfloat16))
        matrix = [matrices[channel // chunk, channel % chunk, tile] for tile in range(tiles)]
        product = jnp.dot(
            jnp.concatenate(pieces, axis=1),
            jnp.concatenate(matrix, axis=1),
            preferred_element_type=jnp.float32,
        )
        keep = height + STEP * (segs - 1)
        total = product[:keep, :LANES]
        for tile in range(1, tiles):
            start = tile * segs * STEP
            total = total + product[start : start + keep, tile * LANES : (tile + 1) * LANES]
        mixed = total[:height, :]
        for seg in range(1, segs):
            part = total[seg * STEP : seg * STEP + height, :]
            mixed = mixed + pltpu.roll(part, LANES - seg * width, axis=1)
        x = shifted[base + half : base + half + height, :]
        result[channel * height : (channel + 1) * height, :] = x + mixed
    lines = []
    for group in range(down * parts):
        line = []
        for start in range(group * taken, (group + 1) * taken, segs):
            value = result[pl.ds(start, count, stride=height), :]
            for seg in range(1, segs):
                other = result[pl.ds(start + seg, count, stride=height), :]
                value = jnp.where(place == seg, pltpu.roll(other, seg * width, axis=1), value)
            line.append(value.astype(jnp.bfloat16))
        lines.append(jnp.concatenate(line, axis=1))
    moved = lax.dot_general(
        jnp.concatenate(lines, axis=0),
        move_ref[...],
        (((1,), (1,)), ((), ())),
        preferred_element_type=jnp.float32,
    )
    for r in range(down):
        for part in range(parts):
            group = r * parts + part
            for c in range(across):
                out_ref[r * across + c, :, part * LANES : (part + 1) * LANES] = moved[
                    group * count : (group + 1) * count, c * LANES : (c + 1) * LANES
                ].astype(out_ref.dtype)


def moves_of(across, tile_cols):
    lane = np.arange(across * LANES)
    step, col = lane % LANES // tile_cols, lane // LANES * tile_cols + lane % tile_cols
    key = jnp.asarray((step * across * tile_cols + col).astype(np.int32))
    cell = lax.broadcasted_iota(jnp.int32, (across * LANES,) * 2, 1)
    return (key[:, None] == cell).astype(jnp.bfloat16)


def spread_moved(matrices, move, received, half, across, tile_cols):
    devices, count, cells = received.shape
    segs = LANES // (across * tile_cols)
    height = devices // across * cells // tile_cols
    tiles = matrices[0].shape[1]
    pitch = height + STEP * tiles * segs
    chunk = per_step(matrices[0].shape[0], CHUNK)
    whole = pl.BlockSpec(memory_space=pltpu.VMEM)
    return pl.pallas_call(
        lambda *refs: moved_kernel(*refs, half=half, segs=segs),
        in_specs=[whole] * 2 + [pl.BlockSpec(memory_space=pl.ANY)] * len(matrices),
        out_specs=whole,
        out_shape=jax.ShapeDtypeStruct(received.shape, received.dtype),
        scratch_shapes=[
            pltpu.VMEM((count * pitch, LANES), jnp.float32),
            pltpu.VMEM((count * height, LANES), jnp.float32),
            pltpu.VMEM((count // chunk, chunk) + matrices[0].shape[1:], matrices[0].dtype),
            pltpu.SemaphoreType.DMA((count // chunk,)),
        ],
        name="depthwise_moved",
    )(received, move, *matrices)


def rows_of(taps, width):
    side, _, count = taps.shape
    segs = LANES // width
    groups = -(-side // (STEP * segs)) * segs
    v = jnp.transpose(taps[:, ::-1, :], (2, 0, 1))
    v = jnp.pad(v, ((0, 0), (0, STEP * groups - side), (0, width - side)))
    v = v.reshape(count, groups, STEP, width).transpose(0, 2, 1, 3)
    return v.reshape(count, STEP, groups // segs, LANES)


def matrices_of(v, part, parts, half, width):
    count = v.shape[0] // parts
    tiles = v.shape[2]
    several = per_step(count, BUILD)
    steps = count // several
    shape = (tiles, STEP * width, LANES)
    size = count * tiles * STEP * width * LANES
    return pl.pallas_call(
        lambda *refs: toeplitz_kernel(*refs, half=half, width=width),
        grid=(steps,),
        in_specs=[
            pl.BlockSpec((several,) + v.shape[1:], lambda i: (i + part * steps, 0, 0, 0))
        ],
        out_specs=pl.BlockSpec((several,) + shape, lambda i: (i, 0, 0, 0)),
        out_shape=jax.ShapeDtypeStruct((count,) + shape, v.dtype),
        cost_estimate=pl.CostEstimate(flops=size * 4, transcendentals=0, bytes_accessed=size * 2),
        name="toeplitz",
    )(v)


def spread_of(matrices, images, half):
    count, height, width = images.shape
    segs = LANES // width
    groups = matrices.shape[1] * segs
    several = per_step(count, CONV)
    return pl.pallas_call(
        lambda *refs: conv_kernel(*refs, half=half, segs=segs),
        grid=(count // several,),
        in_specs=[
            pl.BlockSpec((several,) + matrices.shape[1:], lambda i: (i, 0, 0, 0)),
            pl.BlockSpec((several, height, width), lambda i: (i, 0, 0)),
        ],
        out_specs=pl.BlockSpec((several, height, width), lambda i: (i, 0, 0)),
        out_shape=jax.ShapeDtypeStruct(images.shape, images.dtype),
        scratch_shapes=[pltpu.VMEM((several, height + STEP * groups, LANES), jnp.float32)],
        name="depthwise",
    )(matrices, images)


def add_hidden(total, normed, piece_refs):
    for ref in piece_refs:
        count, _, units, channels = ref.shape
        up = ref[:, 0].reshape(count * units, channels)
        down = ref[:, 1].reshape(count * units, channels)
        hidden = lax.dot_general(
            normed, up, (((1,), (1,)), ((), ())), preferred_element_type=jnp.float32
        )
        hidden = (0.5 * hidden * (1.0 + lax.erf(hidden * 0.5**0.5))).astype(jnp.bfloat16)
        total = total + jnp.dot(hidden, down, preferred_element_type=jnp.float32)
    return total


def first_kernel(*refs):
    spread_ref, *piece_refs, normed_ref, total_ref = refs
    values = spread_ref[...].astype(jnp.float32).T
    center = jnp.mean(values, axis=1, keepdims=True)
    spread_sq = jnp.mean((values - center) ** 2, axis=1, keepdims=True)
    normed = ((values - center) * lax.rsqrt(spread_sq + 1e-06)).astype(jnp.bfloat16)
    normed_ref[...] = normed
    total_ref[...] = add_hidden(values, normed, piece_refs)


def second_kernel(*refs):
    normed_ref, total_ref, *piece_refs, out_ref = refs
    total = add_hidden(total_ref[...], normed_ref[...], piece_refs)
    out_ref[...] = total.astype(out_ref.dtype)


def aligned(pieces):
    channels = pieces[0].shape[3]
    if pieces[0].shape[2] % 16 != 0:
        joined = jnp.concatenate(pieces, axis=0)
        pieces = [joined.transpose(1, 0, 2, 3).reshape(1, 2, -1, channels)]
    return pieces


def block_of(spread, near, far):
    channels, cells = spread.shape
    near, far = aligned(near), aligned(far)
    whole = pl.BlockSpec(memory_space=pltpu.VMEM)
    normed, total = pl.pallas_call(
        first_kernel,
        in_specs=[whole] * (1 + len(near)),
        out_specs=[whole] * 2,
        out_shape=[
            jax.ShapeDtypeStruct((cells, channels), spread.dtype),
            jax.ShapeDtypeStruct((cells, channels), jnp.float32),
        ],
        name="feed_forward_near",
    )(spread, *near)
    return pl.pallas_call(
        second_kernel,
        in_specs=[whole] * (2 + len(far)),
        out_specs=whole,
        out_shape=jax.ShapeDtypeStruct((cells, channels), spread.dtype),
        name="feed_forward_far",
    )(normed, total, *far)


def turn(array, axis, shift, within=1):
    size = lax.axis_size(axis)
    return lax.ppermute(
        array, axis, [(i, (i + shift * within) % size) for i in range(size)]
    )


def partner(array, axis):
    size = lax.axis_size(axis)
    return lax.ppermute(array, axis, [(i, i ^ 1) for i in range(size)])


def on_tile(features, dw_kernel, w_up, w_down):
    axes = ("rows", "cols")
    down = lax.axis_size("rows")
    across = lax.axis_size("cols")
    pages = lax.axis_size("pages")
    devices = down * across
    tile_rows, tile_cols, channels = features.shape
    cells = tile_rows * tile_cols
    own = channels // devices
    half = (dw_kernel.shape[0] - 1) // 2
    units = w_up.shape[1] // pages
    piece = jnp.stack([w_up.T, w_down.T])[None]
    piece = lax.dynamic_slice_in_dim(piece, lax.axis_index("pages") * units, units, axis=2)
    line = [piece] + [turn(piece, "cols", shift) for shift in range(1, across)]
    turned = features.reshape(cells, channels).T.reshape(devices, own, cells)
    images = lax.all_to_all(turned, axes, 0, 0, tiled=True)
    width = across * tile_cols
    taps = rows_of(dw_kernel, width)
    early = matrices_of(taps, 0, 2, half, width)
    early, line = lax.optimization_barrier((early, line))
    line = jnp.concatenate(line, axis=0)
    others = [turn(line, "rows", shift, 2) for shift in range(1, down // 2)]
    near = [line] + [turn(line, "pages", shift) for shift in range(1, pages)]
    late = matrices_of(taps, 1, 2, half, width)
    matrices = [early, late]
    move = moves_of(across, tile_cols)
    images, matrices, move = lax.optimization_barrier((images, matrices, move))
    if own % 16 == 0:
        spread = spread_moved(matrices, move, images, half, across, tile_cols)
    else:
        images = images.reshape(down, across, own, tile_rows, tile_cols)
        images = images.transpose(2, 0, 3, 1, 4)
        images = images.reshape(own, down * tile_rows, across * tile_cols)
        spread = spread_of(jnp.concatenate(matrices, axis=0), images, half)
        spread = spread.reshape(own, down, tile_rows, across, tile_cols)
        spread = spread.transpose(1, 3, 0, 2, 4).reshape(devices, own, cells)
    last = [turn(other, "pages", shift) for other in others for shift in range(1, pages)]
    near = near + others
    far = [partner(each, "rows") for each in near]
    spread = lax.all_to_all(spread, axes, 0, 0, tiled=True)
    spread, last = lax.optimization_barrier((spread, last))
    far += [partner(each, "rows") for each in last]
    result = block_of(spread.reshape(channels, cells), near + last, far)
    return result.reshape(tile_rows, tile_cols, channels)


def solution(mesh):
    return jax.shard_map(
        on_tile,
        mesh=mesh,
        in_specs=(
            P(("pages", "rows"), "cols", None),
            P(None, None, ("rows", "cols")),
            P(None, ("rows", "cols")),
            P(None, ("rows", "cols")),
        ),
        out_specs=P(("pages", "rows"), "cols", None),
        check_vma=False,
    )
```

```python
import jax
import jax.numpy as jnp
import numpy as np
from jax import lax
from jax.experimental import pallas as pl
from jax.experimental.pallas import tpu as pltpu
from jax.sharding import PartitionSpec as P


LANES = 128
STEP = 8
BUILD = 8
CONV = 16
CHUNK = 8


def per_step(count, most):
    return max(n for n in range(1, most + 1) if count % n == 0)


def toeplitz_kernel(v_ref, out_ref, *, half, width):
    count, steps, tiles, _ = v_ref.shape
    block = 16
    lane = lax.broadcasted_iota(jnp.int32, (block, LANES), 1) % width
    row = lax.broadcasted_iota(jnp.int32, (block, LANES), 0)
    bands = [
        jnp.where(jnp.abs(row + start - lane) <= half, 1.0, 0.0).astype(jnp.bfloat16)
        for start in range(0, width, block)
    ]

    def build(channel, carry):
        for shift in range(steps):
            for tile in range(tiles):
                taps = v_ref[channel, shift, tile : tile + 1, :]
                taps = jnp.broadcast_to(taps.astype(jnp.float32), (block, LANES))
                turned = pltpu.roll(taps, LANES - half, axis=1, stride=1, stride_axis=0)
                turned = turned.astype(jnp.bfloat16)
                for index, band in enumerate(bands):
                    start = index * block
                    piece = turned if start == 0 else pltpu.roll(turned, start, axis=1)
                    low = shift * width + start
                    out_ref[channel, tile, low : low + block, :] = piece * band
        return carry

    lax.fori_loop(0, count, build, 0, unroll=per_step(count, 2))


def conv_kernel(matrix_ref, img_ref, out_ref, shifted, *, half, segs):
    count, height, width = img_ref.shape
    tiles = matrix_ref.shape[1]
    rows = height + STEP * (tiles * segs - 1)

    @pl.when(pl.program_id(0) == 0)
    def _():
        shifted[...] = jnp.zeros_like(shifted)

    for channel in range(count):
        x = img_ref[channel].astype(jnp.float32)
        for seg in range(segs):
            shifted[
                channel, half - seg : half - seg + height, seg * width : (seg + 1) * width
            ] = x
        left = jnp.concatenate(
            [
                shifted[channel, s : s + rows, :].astype(jnp.bfloat16)
                for s in range(0, STEP, segs)
            ],
            axis=1,
        )
        matrix = jnp.concatenate([matrix_ref[channel, t] for t in range(tiles)], axis=1)
        product = jnp.dot(left, matrix, preferred_element_type=jnp.float32)
        keep = height + STEP * (segs - 1)
        total = product[:keep, :LANES]
        for tile in range(1, tiles):
            start = tile * segs * STEP
            total = total + product[start : start + keep, tile * LANES : (tile + 1) * LANES]
        mixed = total[:height, :width]
        for seg in range(1, segs):
            part = total[seg * STEP : seg * STEP + height, :]
            mixed = mixed + pltpu.roll(part, LANES - seg * width, axis=1)[:, :width]
        out_ref[channel] = (x + mixed).astype(out_ref.dtype)


def moved_kernel(*refs, half, segs):
    recv_ref, move_ref, *matrix_hbms = refs[:-5]
    out_ref, shifted, result, matrices, sems = refs[-5:]
    count = recv_ref.shape[1]
    across = move_ref.shape[0] // LANES
    parts = recv_ref.shape[2] // LANES
    down = recv_ref.shape[0] // across
    _, chunk, tiles = matrices.shape[:3]
    width = LANES // segs
    taken = move_ref.shape[1] // width
    height = down * parts * taken
    pitch = shifted.shape[0] // count
    rows = height + STEP * (tiles * segs - 1)
    sources = [
        matrix_hbm.at[pl.ds(start, chunk)]
        for matrix_hbm in matrix_hbms
        for start in range(0, matrix_hbm.shape[0], chunk)
    ]
    copies = [
        pltpu.make_async_copy(source, matrices.at[index], sems.at[index])
        for index, source in enumerate(sources)
    ]
    for copy in copies:
        copy.start()
    shifted[...] = jnp.zeros_like(shifted)
    left = jnp.concatenate(
        [
            jnp.concatenate(
                [
                    recv_ref[r * across + c, :, part * LANES : (part + 1) * LANES]
                    for c in range(across)
                ],
                axis=1,
            )
            for r in range(down)
            for part in range(parts)
        ],
        axis=0,
    )
    images = jnp.dot(left, move_ref[...], preferred_element_type=jnp.float32)
    place = lax.broadcasted_iota(jnp.int32, (count, LANES), 1) // width
    for group in range(down * parts):
        for block in range(taken // segs):
            value = images[
                group * count : (group + 1) * count, block * LANES : (block + 1) * LANES
            ]
            for seg in range(segs):
                spot = value
                for other in range(1, segs):
                    moved = pltpu.roll(value, other * width, axis=1)
                    spot = jnp.where(place == (seg + other) % segs, moved, spot)
                row = half + group * taken + block * segs + seg
                shifted[pl.ds(row, count, stride=pitch), :] = spot
    first = lax.broadcasted_iota(jnp.int32, (rows, LANES), 1) // width
    for channel in range(count):
        if channel % chunk == 0:
            copies[channel // chunk].wait()
        base = channel * pitch
        pieces = []
        for shift in range(0, STEP, segs):
            piece = shifted[base + shift : base + shift + rows, :]
            for seg in range(1, segs):
                low = base + shift + seg
                piece = jnp.where(first == seg, shifted[low : low + rows, :], piece)
            pieces.append(piece.astype(jnp.bfloat16))
        matrix = [matrices[channel // chunk, channel % chunk, tile] for tile in range(tiles)]
        product = jnp.dot(
            jnp.concatenate(pieces, axis=1),
            jnp.concatenate(matrix, axis=1),
            preferred_element_type=jnp.float32,
        )
        keep = height + STEP * (segs - 1)
        total = product[:keep, :LANES]
        for tile in range(1, tiles):
            start = tile * segs * STEP
            total = total + product[start : start + keep, tile * LANES : (tile + 1) * LANES]
        mixed = total[:height, :]
        for seg in range(1, segs):
            part = total[seg * STEP : seg * STEP + height, :]
            mixed = mixed + pltpu.roll(part, LANES - seg * width, axis=1)
        x = shifted[base + half : base + half + height, :]
        result[channel * height : (channel + 1) * height, :] = x + mixed
    lines = []
    for group in range(down * parts):
        line = []
        for start in range(group * taken, (group + 1) * taken, segs):
            value = result[pl.ds(start, count, stride=height), :]
            for seg in range(1, segs):
                other = result[pl.ds(start + seg, count, stride=height), :]
                value = jnp.where(place == seg, pltpu.roll(other, seg * width, axis=1), value)
            line.append(value.astype(jnp.bfloat16))
        lines.append(jnp.concatenate(line, axis=1))
    moved = lax.dot_general(
        jnp.concatenate(lines, axis=0),
        move_ref[...],
        (((1,), (1,)), ((), ())),
        preferred_element_type=jnp.float32,
    )
    for r in range(down):
        for part in range(parts):
            group = r * parts + part
            for c in range(across):
                out_ref[r * across + c, :, part * LANES : (part + 1) * LANES] = moved[
                    group * count : (group + 1) * count, c * LANES : (c + 1) * LANES
                ].astype(out_ref.dtype)


def moves_of(across, tile_cols):
    lane = np.arange(across * LANES)
    step, col = lane % LANES // tile_cols, lane // LANES * tile_cols + lane % tile_cols
    key = jnp.asarray((step * across * tile_cols + col).astype(np.int32))
    cell = lax.broadcasted_iota(jnp.int32, (across * LANES,) * 2, 1)
    return (key[:, None] == cell).astype(jnp.bfloat16)


def spread_moved(matrices, move, received, half, across, tile_cols):
    devices, count, cells = received.shape
    segs = LANES // (across * tile_cols)
    height = devices // across * cells // tile_cols
    tiles = matrices[0].shape[1]
    pitch = height + STEP * tiles * segs
    chunk = per_step(matrices[0].shape[0], CHUNK)
    whole = pl.BlockSpec(memory_space=pltpu.VMEM)
    return pl.pallas_call(
        lambda *refs: moved_kernel(*refs, half=half, segs=segs),
        in_specs=[whole] * 2 + [pl.BlockSpec(memory_space=pl.ANY)] * len(matrices),
        out_specs=whole,
        out_shape=jax.ShapeDtypeStruct(received.shape, received.dtype),
        scratch_shapes=[
            pltpu.VMEM((count * pitch, LANES), jnp.float32),
            pltpu.VMEM((count * height, LANES), jnp.float32),
            pltpu.VMEM((count // chunk, chunk) + matrices[0].shape[1:], matrices[0].dtype),
            pltpu.SemaphoreType.DMA((count // chunk,)),
        ],
        name="depthwise_moved",
    )(received, move, *matrices)


def rows_of(taps, width):
    side, _, count = taps.shape
    segs = LANES // width
    groups = -(-side // (STEP * segs)) * segs
    v = jnp.transpose(taps[:, ::-1, :], (2, 0, 1))
    v = jnp.pad(v, ((0, 0), (0, STEP * groups - side), (0, width - side)))
    v = v.reshape(count, groups, STEP, width).transpose(0, 2, 1, 3)
    return v.reshape(count, STEP, groups // segs, LANES)


def matrices_of(v, part, parts, half, width):
    count = v.shape[0] // parts
    tiles = v.shape[2]
    several = per_step(count, BUILD)
    steps = count // several
    shape = (tiles, STEP * width, LANES)
    size = count * tiles * STEP * width * LANES
    return pl.pallas_call(
        lambda *refs: toeplitz_kernel(*refs, half=half, width=width),
        grid=(steps,),
        in_specs=[
            pl.BlockSpec((several,) + v.shape[1:], lambda i: (i + part * steps, 0, 0, 0))
        ],
        out_specs=pl.BlockSpec((several,) + shape, lambda i: (i, 0, 0, 0)),
        out_shape=jax.ShapeDtypeStruct((count,) + shape, v.dtype),
        cost_estimate=pl.CostEstimate(flops=size * 4, transcendentals=0, bytes_accessed=size * 2),
        name="toeplitz",
    )(v)


def spread_of(matrices, images, half):
    count, height, width = images.shape
    segs = LANES // width
    groups = matrices.shape[1] * segs
    several = per_step(count, CONV)
    return pl.pallas_call(
        lambda *refs: conv_kernel(*refs, half=half, segs=segs),
        grid=(count // several,),
        in_specs=[
            pl.BlockSpec((several,) + matrices.shape[1:], lambda i: (i, 0, 0, 0)),
            pl.BlockSpec((several, height, width), lambda i: (i, 0, 0)),
        ],
        out_specs=pl.BlockSpec((several, height, width), lambda i: (i, 0, 0)),
        out_shape=jax.ShapeDtypeStruct(images.shape, images.dtype),
        scratch_shapes=[pltpu.VMEM((several, height + STEP * groups, LANES), jnp.float32)],
        name="depthwise",
    )(matrices, images)


def add_hidden(total, normed, piece_refs):
    channels = normed.shape[1]
    up, down = [
        jnp.concatenate([ref[:, side].reshape(-1, channels) for ref in piece_refs], axis=0)
        for side in range(2)
    ]
    hidden = lax.dot_general(
        normed, up, (((1,), (1,)), ((), ())), preferred_element_type=jnp.float32
    )
    hidden = (0.5 * hidden * (1.0 + lax.erf(hidden * 0.5**0.5))).astype(jnp.bfloat16)
    return total + jnp.dot(hidden, down, preferred_element_type=jnp.float32)


def first_kernel(*refs):
    spread_ref, *piece_refs, normed_ref, total_ref = refs
    values = spread_ref[...].astype(jnp.float32).T
    center = jnp.mean(values, axis=1, keepdims=True)
    spread_sq = jnp.mean((values - center) ** 2, axis=1, keepdims=True)
    normed = ((values - center) * lax.rsqrt(spread_sq + 1e-06)).astype(jnp.bfloat16)
    normed_ref[...] = normed
    total_ref[...] = add_hidden(values, normed, piece_refs)


def second_kernel(*refs):
    normed_ref, total_ref, *piece_refs, out_ref = refs
    total = add_hidden(total_ref[...], normed_ref[...], piece_refs)
    out_ref[...] = total.astype(out_ref.dtype)


def aligned(pieces):
    channels = pieces[0].shape[3]
    if pieces[0].shape[2] % 16 != 0:
        joined = jnp.concatenate(pieces, axis=0)
        pieces = [joined.transpose(1, 0, 2, 3).reshape(1, 2, -1, channels)]
    return pieces


def block_of(spread, near, far):
    channels, cells = spread.shape
    near, far = aligned(near), aligned(far)
    whole = pl.BlockSpec(memory_space=pltpu.VMEM)
    normed, total = pl.pallas_call(
        first_kernel,
        in_specs=[whole] * (1 + len(near)),
        out_specs=[whole] * 2,
        out_shape=[
            jax.ShapeDtypeStruct((cells, channels), spread.dtype),
            jax.ShapeDtypeStruct((cells, channels), jnp.float32),
        ],
        compiler_params=pltpu.CompilerParams(vmem_limit_bytes=16 << 20),
        name="feed_forward_near",
    )(spread, *near)
    return pl.pallas_call(
        second_kernel,
        in_specs=[whole] * (2 + len(far)),
        out_specs=whole,
        out_shape=jax.ShapeDtypeStruct((cells, channels), spread.dtype),
        compiler_params=pltpu.CompilerParams(vmem_limit_bytes=16 << 20),
        name="feed_forward_far",
    )(normed, total, *far)


def turn(array, axis, shift, within=1):
    size = lax.axis_size(axis)
    return lax.ppermute(
        array, axis, [(i, (i + shift * within) % size) for i in range(size)]
    )


def partner(array, axis):
    size = lax.axis_size(axis)
    return lax.ppermute(array, axis, [(i, i ^ 1) for i in range(size)])


def on_tile(features, dw_kernel, w_up, w_down):
    axes = ("rows", "cols")
    down = lax.axis_size("rows")
    across = lax.axis_size("cols")
    pages = lax.axis_size("pages")
    devices = down * across
    tile_rows, tile_cols, channels = features.shape
    cells = tile_rows * tile_cols
    own = channels // devices
    half = (dw_kernel.shape[0] - 1) // 2
    units = w_up.shape[1] // pages
    piece = jnp.stack([w_up.T, w_down.T])[None]
    piece = lax.dynamic_slice_in_dim(piece, lax.axis_index("pages") * units, units, axis=2)
    line = [piece] + [turn(piece, "cols", shift) for shift in range(1, across)]
    turned = features.reshape(cells, channels).T.reshape(devices, own, cells)
    images = lax.all_to_all(turned, axes, 0, 0, tiled=True)
    width = across * tile_cols
    taps = rows_of(dw_kernel, width)
    early = matrices_of(taps, 0, 2, half, width)
    early, line = lax.optimization_barrier((early, line))
    line = jnp.concatenate(line, axis=0)
    others = [turn(line, "rows", shift, 2) for shift in range(1, down // 2)]
    near = [line] + [turn(line, "pages", shift) for shift in range(1, pages)]
    late = matrices_of(taps, 1, 2, half, width)
    matrices = [early, late]
    move = moves_of(across, tile_cols)
    images, matrices, move = lax.optimization_barrier((images, matrices, move))
    if own % 16 == 0:
        spread = spread_moved(matrices, move, images, half, across, tile_cols)
    else:
        images = images.reshape(down, across, own, tile_rows, tile_cols)
        images = images.transpose(2, 0, 3, 1, 4)
        images = images.reshape(own, down * tile_rows, across * tile_cols)
        spread = spread_of(jnp.concatenate(matrices, axis=0), images, half)
        spread = spread.reshape(own, down, tile_rows, across, tile_cols)
        spread = spread.transpose(1, 3, 0, 2, 4).reshape(devices, own, cells)
    last = [turn(other, "pages", shift) for other in others for shift in range(1, pages)]
    near = near + others
    far = [partner(each, "rows") for each in near]
    spread = lax.all_to_all(spread, axes, 0, 0, tiled=True)
    spread, last = lax.optimization_barrier((spread, last))
    far += [partner(each, "rows") for each in last]
    result = block_of(spread.reshape(channels, cells), near + last, far)
    return result.reshape(tile_rows, tile_cols, channels)


def solution(mesh):
    return jax.shard_map(
        on_tile,
        mesh=mesh,
        in_specs=(
            P(("pages", "rows"), "cols", None),
            P(None, None, ("rows", "cols")),
            P(None, ("rows", "cols")),
            P(None, ("rows", "cols")),
        ),
        out_specs=P(("pages", "rows"), "cols", None),
        check_vma=False,
    )
```

```python
import jax
import jax.numpy as jnp
import numpy as np
from jax import lax
from jax.experimental import pallas as pl
from jax.experimental.pallas import tpu as pltpu
from jax.sharding import PartitionSpec as P


LANES = 128
STEP = 8
CONV = 16
CHUNK = 8


def per_step(count, most):
    return max(n for n in range(1, most + 1) if count % n == 0)


def toeplitz_kernel(v_ref, out_hbm, built, sem, *, half, width):
    count, steps, tiles, _ = v_ref.shape
    block = 16
    lane = lax.broadcasted_iota(jnp.int32, (block, LANES), 1) % width
    row = lax.broadcasted_iota(jnp.int32, (block, LANES), 0)
    bands = [
        jnp.where(jnp.abs(row + start - lane) <= half, 1.0, 0.0).astype(jnp.bfloat16)
        for start in range(0, width, block)
    ]

    def build(channel, carry):
        for shift in range(steps):
            for tile in range(tiles):
                taps = v_ref[channel, shift, tile : tile + 1, :]
                taps = jnp.broadcast_to(taps.astype(jnp.float32), (block, LANES))
                turned = pltpu.roll(taps, LANES - half, axis=1, stride=1, stride_axis=0)
                turned = turned.astype(jnp.bfloat16)
                for index, band in enumerate(bands):
                    start = index * block
                    piece = turned if start == 0 else pltpu.roll(turned, start, axis=1)
                    low = shift * width + start
                    built[channel, tile, low : low + block, :] = piece * band
        pltpu.make_async_copy(built.at[channel], out_hbm.at[channel], sem).start()
        return carry

    lax.fori_loop(0, count, build, 0, unroll=per_step(count, 2))
    pltpu.make_async_copy(built, out_hbm, sem).wait()


def conv_kernel(matrix_ref, img_ref, out_ref, shifted, *, half, segs):
    count, height, width = img_ref.shape
    tiles = matrix_ref.shape[1]
    rows = height + STEP * (tiles * segs - 1)

    @pl.when(pl.program_id(0) == 0)
    def _():
        shifted[...] = jnp.zeros_like(shifted)

    for channel in range(count):
        x = img_ref[channel].astype(jnp.float32)
        for seg in range(segs):
            shifted[
                channel, half - seg : half - seg + height, seg * width : (seg + 1) * width
            ] = x
        left = jnp.concatenate(
            [
                shifted[channel, s : s + rows, :].astype(jnp.bfloat16)
                for s in range(0, STEP, segs)
            ],
            axis=1,
        )
        matrix = jnp.concatenate([matrix_ref[channel, t] for t in range(tiles)], axis=1)
        product = jnp.dot(left, matrix, preferred_element_type=jnp.float32)
        keep = height + STEP * (segs - 1)
        total = product[:keep, :LANES]
        for tile in range(1, tiles):
            start = tile * segs * STEP
            total = total + product[start : start + keep, tile * LANES : (tile + 1) * LANES]
        mixed = total[:height, :width]
        for seg in range(1, segs):
            part = total[seg * STEP : seg * STEP + height, :]
            mixed = mixed + pltpu.roll(part, LANES - seg * width, axis=1)[:, :width]
        out_ref[channel] = (x + mixed).astype(out_ref.dtype)


def moved_kernel(*refs, half, segs):
    recv_ref, move_ref, *matrix_hbms = refs[:-5]
    out_ref, shifted, result, matrices, sems = refs[-5:]
    count = recv_ref.shape[1]
    across = move_ref.shape[0] // LANES
    parts = recv_ref.shape[2] // LANES
    down = recv_ref.shape[0] // across
    _, chunk, tiles = matrices.shape[:3]
    width = LANES // segs
    taken = move_ref.shape[1] // width
    height = down * parts * taken
    pitch = shifted.shape[0] // count
    rows = height + STEP * (tiles * segs - 1)
    sources = [
        matrix_hbm.at[pl.ds(start, chunk)]
        for matrix_hbm in matrix_hbms
        for start in range(0, matrix_hbm.shape[0], chunk)
    ]
    copies = [
        pltpu.make_async_copy(source, matrices.at[index], sems.at[index])
        for index, source in enumerate(sources)
    ]
    for copy in copies:
        copy.start()
    shifted[...] = jnp.zeros_like(shifted)
    left = jnp.concatenate(
        [
            jnp.concatenate(
                [
                    recv_ref[r * across + c, :, part * LANES : (part + 1) * LANES]
                    for c in range(across)
                ],
                axis=1,
            )
            for r in range(down)
            for part in range(parts)
        ],
        axis=0,
    )
    images = jnp.dot(left, move_ref[...], preferred_element_type=jnp.float32)
    place = lax.broadcasted_iota(jnp.int32, (count, LANES), 1) // width
    for group in range(down * parts):
        for block in range(taken // segs):
            value = images[
                group * count : (group + 1) * count, block * LANES : (block + 1) * LANES
            ]
            for seg in range(segs):
                spot = value
                for other in range(1, segs):
                    moved = pltpu.roll(value, other * width, axis=1)
                    spot = jnp.where(place == (seg + other) % segs, moved, spot)
                row = half + group * taken + block * segs + seg
                shifted[pl.ds(row, count, stride=pitch), :] = spot
    first = lax.broadcasted_iota(jnp.int32, (rows, LANES), 1) // width
    for channel in range(count):
        if channel % chunk == 0:
            copies[channel // chunk].wait()
        base = channel * pitch
        pieces = []
        for shift in range(0, STEP, segs):
            piece = shifted[base + shift : base + shift + rows, :]
            for seg in range(1, segs):
                low = base + shift + seg
                piece = jnp.where(first == seg, shifted[low : low + rows, :], piece)
            pieces.append(piece.astype(jnp.bfloat16))
        matrix = [matrices[channel // chunk, channel % chunk, tile] for tile in range(tiles)]
        product = jnp.dot(
            jnp.concatenate(pieces, axis=1),
            jnp.concatenate(matrix, axis=1),
            preferred_element_type=jnp.float32,
        )
        keep = height + STEP * (segs - 1)
        total = product[:keep, :LANES]
        for tile in range(1, tiles):
            start = tile * segs * STEP
            total = total + product[start : start + keep, tile * LANES : (tile + 1) * LANES]
        mixed = total[:height, :]
        for seg in range(1, segs):
            part = total[seg * STEP : seg * STEP + height, :]
            mixed = mixed + pltpu.roll(part, LANES - seg * width, axis=1)
        x = shifted[base + half : base + half + height, :]
        result[channel * height : (channel + 1) * height, :] = x + mixed
    lines = []
    for group in range(down * parts):
        line = []
        for start in range(group * taken, (group + 1) * taken, segs):
            value = result[pl.ds(start, count, stride=height), :]
            for seg in range(1, segs):
                other = result[pl.ds(start + seg, count, stride=height), :]
                value = jnp.where(place == seg, pltpu.roll(other, seg * width, axis=1), value)
            line.append(value.astype(jnp.bfloat16))
        lines.append(jnp.concatenate(line, axis=1))
    moved = lax.dot_general(
        jnp.concatenate(lines, axis=0),
        move_ref[...],
        (((1,), (1,)), ((), ())),
        preferred_element_type=jnp.float32,
    )
    for r in range(down):
        for part in range(parts):
            group = r * parts + part
            for c in range(across):
                out_ref[r * across + c, :, part * LANES : (part + 1) * LANES] = moved[
                    group * count : (group + 1) * count, c * LANES : (c + 1) * LANES
                ].astype(out_ref.dtype)


def moves_of(across, tile_cols):
    lane = np.arange(across * LANES)
    step, col = lane % LANES // tile_cols, lane // LANES * tile_cols + lane % tile_cols
    key = jnp.asarray((step * across * tile_cols + col).astype(np.int32))
    cell = lax.broadcasted_iota(jnp.int32, (across * LANES,) * 2, 1)
    return (key[:, None] == cell).astype(jnp.bfloat16)


def spread_moved(matrices, move, received, half, across, tile_cols):
    devices, count, cells = received.shape
    segs = LANES // (across * tile_cols)
    height = devices // across * cells // tile_cols
    tiles = matrices[0].shape[1]
    pitch = height + STEP * tiles * segs
    chunk = per_step(matrices[0].shape[0], CHUNK)
    whole = pl.BlockSpec(memory_space=pltpu.VMEM)
    return pl.pallas_call(
        lambda *refs: moved_kernel(*refs, half=half, segs=segs),
        in_specs=[whole] * 2 + [pl.BlockSpec(memory_space=pl.ANY)] * len(matrices),
        out_specs=whole,
        out_shape=jax.ShapeDtypeStruct(received.shape, received.dtype),
        scratch_shapes=[
            pltpu.VMEM((count * pitch, LANES), jnp.float32),
            pltpu.VMEM((count * height, LANES), jnp.float32),
            pltpu.VMEM((count // chunk, chunk) + matrices[0].shape[1:], matrices[0].dtype),
            pltpu.SemaphoreType.DMA((count // chunk,)),
        ],
        name="depthwise_moved",
    )(received, move, *matrices)


def rows_of(taps, width):
    side, _, count = taps.shape
    segs = LANES // width
    groups = -(-side // (STEP * segs)) * segs
    v = jnp.transpose(taps[:, ::-1, :], (2, 0, 1))
    v = jnp.pad(v, ((0, 0), (0, STEP * groups - side), (0, width - side)))
    v = v.reshape(count, groups, STEP, width).transpose(0, 2, 1, 3)
    return v.reshape(count, STEP, groups // segs, LANES)


def matrices_of(v, part, parts, half, width):
    count = v.shape[0] // parts
    tiles = v.shape[2]
    shape = (count, tiles, STEP * width, LANES)
    size = count * tiles * STEP * width * LANES
    return pl.pallas_call(
        lambda *refs: toeplitz_kernel(*refs, half=half, width=width),
        grid=(1,),
        in_specs=[pl.BlockSpec((count,) + v.shape[1:], lambda i: (part, 0, 0, 0))],
        out_specs=pl.BlockSpec(memory_space=pl.ANY),
        out_shape=jax.ShapeDtypeStruct(shape, v.dtype),
        scratch_shapes=[pltpu.VMEM(shape, v.dtype), pltpu.SemaphoreType.DMA(())],
        cost_estimate=pl.CostEstimate(flops=size * 4, transcendentals=0, bytes_accessed=size * 2),
        name="toeplitz",
    )(v)


def spread_of(matrices, images, half):
    count, height, width = images.shape
    segs = LANES // width
    groups = matrices.shape[1] * segs
    several = per_step(count, CONV)
    return pl.pallas_call(
        lambda *refs: conv_kernel(*refs, half=half, segs=segs),
        grid=(count // several,),
        in_specs=[
            pl.BlockSpec((several,) + matrices.shape[1:], lambda i: (i, 0, 0, 0)),
            pl.BlockSpec((several, height, width), lambda i: (i, 0, 0)),
        ],
        out_specs=pl.BlockSpec((several, height, width), lambda i: (i, 0, 0)),
        out_shape=jax.ShapeDtypeStruct(images.shape, images.dtype),
        scratch_shapes=[pltpu.VMEM((several, height + STEP * groups, LANES), jnp.float32)],
        name="depthwise",
    )(matrices, images)


def add_hidden(total, normed, piece_refs):
    channels = normed.shape[1]
    up, down = [
        jnp.concatenate([ref[:, side].reshape(-1, channels) for ref in piece_refs], axis=0)
        for side in range(2)
    ]
    hidden = lax.dot_general(
        normed, up, (((1,), (1,)), ((), ())), preferred_element_type=jnp.float32
    )
    hidden = (0.5 * hidden * (1.0 + lax.erf(hidden * 0.5**0.5))).astype(jnp.bfloat16)
    return total + jnp.dot(hidden, down, preferred_element_type=jnp.float32)


def first_kernel(*refs):
    spread_ref, *piece_refs, normed_ref, total_ref = refs
    values = spread_ref[...].astype(jnp.float32).T
    center = jnp.mean(values, axis=1, keepdims=True)
    spread_sq = jnp.mean((values - center) ** 2, axis=1, keepdims=True)
    normed = ((values - center) * lax.rsqrt(spread_sq + 1e-06)).astype(jnp.bfloat16)
    normed_ref[...] = normed
    total_ref[...] = add_hidden(values, normed, piece_refs)


def second_kernel(*refs):
    normed_ref, total_ref, *piece_refs, out_ref = refs
    total = add_hidden(total_ref[...], normed_ref[...], piece_refs)
    out_ref[...] = total.astype(out_ref.dtype)


def aligned(pieces):
    channels = pieces[0].shape[3]
    if pieces[0].shape[2] % 16 != 0:
        joined = jnp.concatenate(pieces, axis=0)
        pieces = [joined.transpose(1, 0, 2, 3).reshape(1, 2, -1, channels)]
    return pieces


def block_of(spread, near, far):
    channels, cells = spread.shape
    near, far = aligned(near), aligned(far)
    whole = pl.BlockSpec(memory_space=pltpu.VMEM)
    normed, total = pl.pallas_call(
        first_kernel,
        in_specs=[whole] * (1 + len(near)),
        out_specs=[whole] * 2,
        out_shape=[
            jax.ShapeDtypeStruct((cells, channels), spread.dtype),
            jax.ShapeDtypeStruct((cells, channels), jnp.float32),
        ],
        compiler_params=pltpu.CompilerParams(vmem_limit_bytes=16 << 20),
        name="feed_forward_near",
    )(spread, *near)
    return pl.pallas_call(
        second_kernel,
        in_specs=[whole] * (2 + len(far)),
        out_specs=whole,
        out_shape=jax.ShapeDtypeStruct((cells, channels), spread.dtype),
        compiler_params=pltpu.CompilerParams(vmem_limit_bytes=16 << 20),
        name="feed_forward_far",
    )(normed, total, *far)


def turn(array, axis, shift, within=1):
    size = lax.axis_size(axis)
    return lax.ppermute(
        array, axis, [(i, (i + shift * within) % size) for i in range(size)]
    )


def partner(array, axis):
    size = lax.axis_size(axis)
    return lax.ppermute(array, axis, [(i, i ^ 1) for i in range(size)])


def on_tile(features, dw_kernel, w_up, w_down):
    axes = ("rows", "cols")
    down = lax.axis_size("rows")
    across = lax.axis_size("cols")
    pages = lax.axis_size("pages")
    devices = down * across
    tile_rows, tile_cols, channels = features.shape
    cells = tile_rows * tile_cols
    own = channels // devices
    half = (dw_kernel.shape[0] - 1) // 2
    units = w_up.shape[1] // pages
    piece = jnp.stack([w_up.T, w_down.T])[None]
    piece = lax.dynamic_slice_in_dim(piece, lax.axis_index("pages") * units, units, axis=2)
    line = [piece] + [turn(piece, "cols", shift) for shift in range(1, across)]
    turned = features.reshape(cells, channels).T.reshape(devices, own, cells)
    images = lax.all_to_all(turned, axes, 0, 0, tiled=True)
    width = across * tile_cols
    taps = rows_of(dw_kernel, width)
    early = matrices_of(taps, 0, 2, half, width)
    early, line = lax.optimization_barrier((early, line))
    line = jnp.concatenate(line, axis=0)
    others = [turn(line, "rows", shift, 2) for shift in range(1, down // 2)]
    near = [line] + [turn(line, "pages", shift) for shift in range(1, pages)]
    late = matrices_of(taps, 1, 2, half, width)
    matrices = [early, late]
    move = moves_of(across, tile_cols)
    images, matrices, move = lax.optimization_barrier((images, matrices, move))
    if own % 16 == 0:
        spread = spread_moved(matrices, move, images, half, across, tile_cols)
    else:
        images = images.reshape(down, across, own, tile_rows, tile_cols)
        images = images.transpose(2, 0, 3, 1, 4)
        images = images.reshape(own, down * tile_rows, across * tile_cols)
        spread = spread_of(jnp.concatenate(matrices, axis=0), images, half)
        spread = spread.reshape(own, down, tile_rows, across, tile_cols)
        spread = spread.transpose(1, 3, 0, 2, 4).reshape(devices, own, cells)
    last = [turn(other, "pages", shift) for other in others for shift in range(1, pages)]
    near = near + others
    far = [partner(each, "rows") for each in near]
    spread = lax.all_to_all(spread, axes, 0, 0, tiled=True)
    spread, last = lax.optimization_barrier((spread, last))
    far += [partner(each, "rows") for each in last]
    result = block_of(spread.reshape(channels, cells), near + last, far)
    return result.reshape(tile_rows, tile_cols, channels)


def solution(mesh):
    return jax.shard_map(
        on_tile,
        mesh=mesh,
        in_specs=(
            P(("pages", "rows"), "cols", None),
            P(None, None, ("rows", "cols")),
            P(None, ("rows", "cols")),
            P(None, ("rows", "cols")),
        ),
        out_specs=P(("pages", "rows"), "cols", None),
        check_vma=False,
    )
```

```python
import jax
import jax.numpy as jnp
import numpy as np
from jax import lax
from jax.experimental import pallas as pl
from jax.experimental.pallas import tpu as pltpu
from jax.sharding import PartitionSpec as P


LANES = 128
STEP = 8
CONV = 16
CHUNK = 8


def per_step(count, most):
    return max(n for n in range(1, most + 1) if count % n == 0)


def toeplitz_kernel(v_ref, out_hbm, built, sem, *, half, width):
    count, steps, tiles, _ = v_ref.shape
    block = 16
    lane = lax.broadcasted_iota(jnp.int32, (block, LANES), 1) % width
    row = lax.broadcasted_iota(jnp.int32, (block, LANES), 0)
    bands = [
        jnp.where(jnp.abs(row + start - lane) <= half, 1.0, 0.0).astype(jnp.bfloat16)
        for start in range(0, width, block)
    ]

    def build(channel, carry):
        for shift in range(steps):
            for tile in range(tiles):
                taps = v_ref[channel, shift, tile : tile + 1, :]
                taps = jnp.broadcast_to(taps.astype(jnp.float32), (block, LANES))
                turned = pltpu.roll(taps, LANES - half, axis=1, stride=1, stride_axis=0)
                turned = turned.astype(jnp.bfloat16)
                for index, band in enumerate(bands):
                    start = index * block
                    piece = turned if start == 0 else pltpu.roll(turned, start, axis=1)
                    low = shift * width + start
                    built[channel, tile, low : low + block, :] = piece * band
        pltpu.make_async_copy(built.at[channel], out_hbm.at[channel], sem).start()
        return carry

    lax.fori_loop(0, count, build, 0, unroll=per_step(count, 2))
    pltpu.make_async_copy(built, out_hbm, sem).wait()


def conv_kernel(matrix_ref, img_ref, out_ref, shifted, *, half, segs):
    count, height, width = img_ref.shape
    tiles = matrix_ref.shape[1]
    rows = height + STEP * (tiles * segs - 1)

    @pl.when(pl.program_id(0) == 0)
    def _():
        shifted[...] = jnp.zeros_like(shifted)

    for channel in range(count):
        x = img_ref[channel].astype(jnp.float32)
        for seg in range(segs):
            shifted[
                channel, half - seg : half - seg + height, seg * width : (seg + 1) * width
            ] = x
        left = jnp.concatenate(
            [
                shifted[channel, s : s + rows, :].astype(jnp.bfloat16)
                for s in range(0, STEP, segs)
            ],
            axis=1,
        )
        matrix = jnp.concatenate([matrix_ref[channel, t] for t in range(tiles)], axis=1)
        product = jnp.dot(left, matrix, preferred_element_type=jnp.float32)
        keep = height + STEP * (segs - 1)
        total = product[:keep, :LANES]
        for tile in range(1, tiles):
            start = tile * segs * STEP
            total = total + product[start : start + keep, tile * LANES : (tile + 1) * LANES]
        mixed = total[:height, :width]
        for seg in range(1, segs):
            part = total[seg * STEP : seg * STEP + height, :]
            mixed = mixed + pltpu.roll(part, LANES - seg * width, axis=1)[:, :width]
        out_ref[channel] = (x + mixed).astype(out_ref.dtype)


def moved_kernel(*refs, half, segs):
    recv_ref, move_ref, *matrix_hbms = refs[:-5]
    out_ref, shifted, result, matrices, sems = refs[-5:]
    count = recv_ref.shape[1]
    across = move_ref.shape[0] // LANES
    parts = recv_ref.shape[2] // LANES
    down = recv_ref.shape[0] // across
    _, chunk, tiles = matrices.shape[:3]
    width = LANES // segs
    taken = move_ref.shape[1] // width
    height = down * parts * taken
    pitch = shifted.shape[0] // count
    rows = height + STEP * (tiles * segs - 1)
    sources = [
        matrix_hbm.at[pl.ds(start, chunk)]
        for matrix_hbm in matrix_hbms
        for start in range(0, matrix_hbm.shape[0], chunk)
    ]
    copies = [
        pltpu.make_async_copy(source, matrices.at[index], sems.at[index])
        for index, source in enumerate(sources)
    ]
    for copy in copies:
        copy.start()
    shifted[...] = jnp.zeros_like(shifted)
    left = jnp.concatenate(
        [
            jnp.concatenate(
                [
                    recv_ref[r * across + c, :, part * LANES : (part + 1) * LANES]
                    for c in range(across)
                ],
                axis=1,
            )
            for r in range(down)
            for part in range(parts)
        ],
        axis=0,
    )
    images = jnp.dot(left, move_ref[...], preferred_element_type=jnp.float32)
    place = lax.broadcasted_iota(jnp.int32, (count, LANES), 1) // width
    for group in range(down * parts):
        for block in range(taken // segs):
            value = images[
                group * count : (group + 1) * count, block * LANES : (block + 1) * LANES
            ]
            for seg in range(segs):
                spot = value
                for other in range(1, segs):
                    moved = pltpu.roll(value, other * width, axis=1)
                    spot = jnp.where(place == (seg + other) % segs, moved, spot)
                row = half + group * taken + block * segs + seg
                shifted[pl.ds(row, count, stride=pitch), :] = spot
    first = lax.broadcasted_iota(jnp.int32, (rows, LANES), 1) // width
    for channel in range(count):
        if channel % chunk == 0:
            copies[channel // chunk].wait()
        base = channel * pitch
        pieces = []
        for shift in range(0, STEP, segs):
            piece = shifted[base + shift : base + shift + rows, :]
            for seg in range(1, segs):
                low = base + shift + seg
                piece = jnp.where(first == seg, shifted[low : low + rows, :], piece)
            pieces.append(piece.astype(jnp.bfloat16))
        matrix = [matrices[channel // chunk, channel % chunk, tile] for tile in range(tiles)]
        product = jnp.dot(
            jnp.concatenate(pieces, axis=1),
            jnp.concatenate(matrix, axis=1),
            preferred_element_type=jnp.float32,
        )
        keep = height + STEP * (segs - 1)
        total = product[:keep, :LANES]
        for tile in range(1, tiles):
            start = tile * segs * STEP
            total = total + product[start : start + keep, tile * LANES : (tile + 1) * LANES]
        mixed = total[:height, :]
        for seg in range(1, segs):
            part = total[seg * STEP : seg * STEP + height, :]
            mixed = mixed + pltpu.roll(part, LANES - seg * width, axis=1)
        x = shifted[base + half : base + half + height, :]
        result[channel * height : (channel + 1) * height, :] = x + mixed
    lines = []
    for group in range(down * parts):
        line = []
        for start in range(group * taken, (group + 1) * taken, segs):
            value = result[pl.ds(start, count, stride=height), :]
            for seg in range(1, segs):
                other = result[pl.ds(start + seg, count, stride=height), :]
                value = jnp.where(place == seg, pltpu.roll(other, seg * width, axis=1), value)
            line.append(value.astype(jnp.bfloat16))
        lines.append(jnp.concatenate(line, axis=1))
    moved = lax.dot_general(
        jnp.concatenate(lines, axis=0),
        move_ref[...],
        (((1,), (1,)), ((), ())),
        preferred_element_type=jnp.float32,
    )
    for r in range(down):
        for part in range(parts):
            group = r * parts + part
            for c in range(across):
                out_ref[r * across + c, :, part * LANES : (part + 1) * LANES] = moved[
                    group * count : (group + 1) * count, c * LANES : (c + 1) * LANES
                ].astype(out_ref.dtype)


def moves_of(across, tile_cols):
    lane = np.arange(across * LANES)
    step, col = lane % LANES // tile_cols, lane // LANES * tile_cols + lane % tile_cols
    key = jnp.asarray((step * across * tile_cols + col).astype(np.int32))
    cell = lax.broadcasted_iota(jnp.int32, (across * LANES,) * 2, 1)
    return (key[:, None] == cell).astype(jnp.bfloat16)


def spread_moved(matrices, move, received, half, across, tile_cols):
    devices, count, cells = received.shape
    segs = LANES // (across * tile_cols)
    height = devices // across * cells // tile_cols
    tiles = matrices[0].shape[1]
    pitch = height + STEP * tiles * segs
    chunk = per_step(matrices[0].shape[0], CHUNK)
    whole = pl.BlockSpec(memory_space=pltpu.VMEM)
    return pl.pallas_call(
        lambda *refs: moved_kernel(*refs, half=half, segs=segs),
        in_specs=[whole] * 2 + [pl.BlockSpec(memory_space=pl.ANY)] * len(matrices),
        out_specs=whole,
        out_shape=jax.ShapeDtypeStruct(received.shape, received.dtype),
        scratch_shapes=[
            pltpu.VMEM((count * pitch, LANES), jnp.float32),
            pltpu.VMEM((count * height, LANES), jnp.float32),
            pltpu.VMEM((count // chunk, chunk) + matrices[0].shape[1:], matrices[0].dtype),
            pltpu.SemaphoreType.DMA((count // chunk,)),
        ],
        name="depthwise_moved",
    )(received, move, *matrices)


def rows_of(taps, width):
    side, _, count = taps.shape
    segs = LANES // width
    groups = -(-side // (STEP * segs)) * segs
    v = jnp.transpose(taps[:, ::-1, :], (2, 0, 1))
    v = jnp.pad(v, ((0, 0), (0, STEP * groups - side), (0, width - side)))
    v = v.reshape(count, groups, STEP, width).transpose(0, 2, 1, 3)
    return v.reshape(count, STEP, groups // segs, LANES)


def matrices_of(v, part, parts, half, width):
    count = v.shape[0] // parts
    tiles = v.shape[2]
    shape = (count, tiles, STEP * width, LANES)
    size = count * tiles * STEP * width * LANES
    return pl.pallas_call(
        lambda *refs: toeplitz_kernel(*refs, half=half, width=width),
        grid=(1,),
        in_specs=[pl.BlockSpec((count,) + v.shape[1:], lambda i: (part, 0, 0, 0))],
        out_specs=pl.BlockSpec(memory_space=pl.ANY),
        out_shape=jax.ShapeDtypeStruct(shape, v.dtype),
        scratch_shapes=[pltpu.VMEM(shape, v.dtype), pltpu.SemaphoreType.DMA(())],
        cost_estimate=pl.CostEstimate(flops=size * 4, transcendentals=0, bytes_accessed=size * 2),
        name="toeplitz",
    )(v)


def spread_of(matrices, images, half):
    count, height, width = images.shape
    segs = LANES // width
    groups = matrices.shape[1] * segs
    several = per_step(count, CONV)
    return pl.pallas_call(
        lambda *refs: conv_kernel(*refs, half=half, segs=segs),
        grid=(count // several,),
        in_specs=[
            pl.BlockSpec((several,) + matrices.shape[1:], lambda i: (i, 0, 0, 0)),
            pl.BlockSpec((several, height, width), lambda i: (i, 0, 0)),
        ],
        out_specs=pl.BlockSpec((several, height, width), lambda i: (i, 0, 0)),
        out_shape=jax.ShapeDtypeStruct(images.shape, images.dtype),
        scratch_shapes=[pltpu.VMEM((several, height + STEP * groups, LANES), jnp.float32)],
        name="depthwise",
    )(matrices, images)


def add_hidden(total, normed, piece_refs):
    channels = normed.shape[1]
    up, down = [
        jnp.concatenate([ref[:, side].reshape(-1, channels) for ref in piece_refs], axis=0)
        for side in range(2)
    ]
    hidden = lax.dot_general(
        normed, up, (((1,), (1,)), ((), ())), preferred_element_type=jnp.float32
    )
    hidden = (0.5 * hidden * (1.0 + lax.erf(hidden * 0.5**0.5))).astype(jnp.bfloat16)
    return total + jnp.dot(hidden, down, preferred_element_type=jnp.float32)


def first_kernel(*refs):
    spread_ref, *piece_refs, normed_ref, total_ref = refs
    values = spread_ref[...].astype(jnp.float32).T
    center = jnp.mean(values, axis=1, keepdims=True)
    spread_sq = jnp.mean((values - center) ** 2, axis=1, keepdims=True)
    normed = ((values - center) * lax.rsqrt(spread_sq + 1e-06)).astype(jnp.bfloat16)
    normed_ref[...] = normed
    total_ref[...] = add_hidden(values, normed, piece_refs)


def second_kernel(*refs):
    normed_ref, total_ref, *piece_refs, out_ref = refs
    total = add_hidden(total_ref[...], normed_ref[...], piece_refs)
    out_ref[...] = total.astype(out_ref.dtype)


def aligned(pieces):
    channels = pieces[0].shape[3]
    if pieces[0].shape[2] % 16 != 0:
        joined = jnp.concatenate(pieces, axis=0)
        pieces = [joined.transpose(1, 0, 2, 3).reshape(1, 2, -1, channels)]
    return pieces


def block_of(spread, near, far):
    channels, cells = spread.shape
    near, far = aligned(near), aligned(far)
    whole = pl.BlockSpec(memory_space=pltpu.VMEM)
    normed, total = pl.pallas_call(
        first_kernel,
        in_specs=[whole] * (1 + len(near)),
        out_specs=[whole] * 2,
        out_shape=[
            jax.ShapeDtypeStruct((cells, channels), spread.dtype),
            jax.ShapeDtypeStruct((cells, channels), jnp.float32),
        ],
        compiler_params=pltpu.CompilerParams(vmem_limit_bytes=16 << 20),
        name="feed_forward_near",
    )(spread, *near)
    return pl.pallas_call(
        second_kernel,
        in_specs=[whole] * (2 + len(far)),
        out_specs=whole,
        out_shape=jax.ShapeDtypeStruct((cells, channels), spread.dtype),
        compiler_params=pltpu.CompilerParams(vmem_limit_bytes=16 << 20),
        name="feed_forward_far",
    )(normed, total, *far)


def turn(array, axis, shift, within=1):
    size = lax.axis_size(axis)
    return lax.ppermute(
        array, axis, [(i, (i + shift * within) % size) for i in range(size)]
    )


def partner(array, axis):
    size = lax.axis_size(axis)
    return lax.ppermute(array, axis, [(i, i ^ 1) for i in range(size)])


def on_tile(features, dw_kernel, w_up, w_down):
    axes = ("rows", "cols")
    down = lax.axis_size("rows")
    across = lax.axis_size("cols")
    pages = lax.axis_size("pages")
    devices = down * across
    tile_rows, tile_cols, channels = features.shape
    cells = tile_rows * tile_cols
    own = channels // devices
    half = (dw_kernel.shape[0] - 1) // 2
    units = w_up.shape[1] // pages
    piece = jnp.stack([w_up.T, w_down.T])[None]
    piece = lax.dynamic_slice_in_dim(piece, lax.axis_index("pages") * units, units, axis=2)
    line = [piece] + [turn(piece, "cols", shift) for shift in range(1, across)]
    turned = features.reshape(cells, channels).T.reshape(devices, own, cells)
    images = lax.all_to_all(turned, axes, 0, 0, tiled=True)
    width = across * tile_cols
    taps = rows_of(dw_kernel, width)
    early = matrices_of(taps, 0, 2, half, width)
    early, line = lax.optimization_barrier((early, line))
    line = jnp.concatenate(line, axis=0)
    others = [turn(line, "rows", shift, 2) for shift in range(1, down // 2)]
    near = [line] + [turn(line, "pages", shift) for shift in range(1, pages)]
    late = matrices_of(taps, 1, 2, half, width)
    matrices = [early, late]
    move = moves_of(across, tile_cols)
    images, matrices, move = lax.optimization_barrier((images, matrices, move))
    if own % 16 == 0:
        spread = spread_moved(matrices, move, images, half, across, tile_cols)
    else:
        images = images.reshape(down, across, own, tile_rows, tile_cols)
        images = images.transpose(2, 0, 3, 1, 4)
        images = images.reshape(own, down * tile_rows, across * tile_cols)
        spread = spread_of(jnp.concatenate(matrices, axis=0), images, half)
        spread = spread.reshape(own, down, tile_rows, across, tile_cols)
        spread = spread.transpose(1, 3, 0, 2, 4).reshape(devices, own, cells)
    last = [turn(other, "pages", shift) for other in others for shift in range(1, pages)]
    near = near + others
    far = [partner(each, "rows") for each in near]
    spread = lax.all_to_all(spread, axes, 0, 0, tiled=True)
    spread, last = lax.optimization_barrier((spread, last))
    near = near + last + far
    far = [partner(each, "rows") for each in last]
    result = block_of(spread.reshape(channels, cells), near, far)
    return result.reshape(tile_rows, tile_cols, channels)


def solution(mesh):
    return jax.shard_map(
        on_tile,
        mesh=mesh,
        in_specs=(
            P(("pages", "rows"), "cols", None),
            P(None, None, ("rows", "cols")),
            P(None, ("rows", "cols")),
            P(None, ("rows", "cols")),
        ),
        out_specs=P(("pages", "rows"), "cols", None),
        check_vma=False,
    )
```
